512 devices in a mesh: tm: 32 (over x, z), space: 16 (over y, core).
Axes of the slice: x: 4, y: 8, z: 8, core: 2. Of those that a mesh axis runs over, the one named last changes fastest.
Arguments:
- slice_starts: float32 [32, 3, 256, 32, 128], P('tm', None, 'space'), may hold values from -6 to 6
- fine_ends: float32 [32, 3, 256, 32, 128], P('tm', None, 'space'), may hold values from -6 to 6
- level_speeds: float32 [2, 128], replicated, may hold values from -0.15 to 0.15
Outputs:
- new_starts: float32 [32, 3, 256, 32, 128], P('tm', None, 'space')
- fine_jumps: float32 [32, 3, 256, 32, 128], P('tm', None, 'space')
The draws below stay inside these ranges and needn't reach their ends.
All inputs are finite; a program needn't handle non-finite values.
Results may differ from the reference program's by a relative error of at most 0.00029.
Values sent between devices are 32-bit elements; how exact they have to be, the bound alone decides.
No kernel may reach another device: no remote copies, remote signals or barrier semaphores. Data moves between devices by JAX's collectives and lax.ppermute only.
A program may use at most 64 MiB of HBM per device.

```python
import math
import jax
import jax.numpy as jnp
from jax import lax

NZ = 128
STEPS = 4
SLICES = 32
NX = 256
NY = 32


def slice_fields(key, shared_key):
    keys = jax.random.split(key, 8)
    shared_keys = jax.random.split(shared_key, 2)
    shape = (SLICES, 3, NX, NY, NZ)
    column_scale = jnp.exp(jax.random.uniform(shared_keys[0], (1, 1, NX, 1, 1), jnp.float32, math.log(0.3), math.log(3.0)))
    slice_scale = jnp.exp(jax.random.uniform(keys[3], (SLICES, 1, 1, 1, 1), jnp.float32, math.log(0.5), math.log(2.0)))
    common_weight = jax.random.uniform(keys[4], (SLICES, 1, 1, 1, 1), jnp.float32, 0.3, 1.0)
    wave_x = jax.random.randint(keys[5], (SLICES, 3, 1, 1, 1), 1, 4).astype(jnp.float32)
    wave_y = jax.random.randint(keys[6], (SLICES, 3, 1, 1, 1), 1, 4).astype(jnp.float32)
    phase = jax.random.uniform(keys[7], (SLICES, 3, 1, 1, NZ), jnp.float32, -math.pi, math.pi)
    x_frac = (jnp.arange(NX, dtype=jnp.float32) / NX).reshape(1, 1, NX, 1, 1)
    y_frac = (jnp.arange(NY, dtype=jnp.float32) / NY).reshape(1, 1, 1, NY, 1)
    wave = jnp.cos(2.0 * math.pi * (wave_x * x_frac + wave_y * y_frac) + phase)
    rough = jax.random.uniform(keys[0], shape, jnp.float32, -1.0, 1.0)
    common = jax.random.uniform(shared_keys[1], (1, 3, NX, NY, NZ), jnp.float32, -1.0, 1.0)
    smooth = wave
    return slice_scale * (0.6 * column_scale * rough + 0.6 * common_weight * common + 0.5 * smooth)


def draw_slice_starts(key, part):
    return slice_fields(jax.random.fold_in(key, 11), jax.random.fold_in(key, 17))


def draw_fine_ends(key, part):
    return slice_fields(jax.random.fold_in(key, 13), jax.random.fold_in(key, 17))


def setup_inputs(seed: int = 0) -> dict:
    arg_keys = jax.random.split(jax.random.key(seed), 4)
    return {
        "slice_starts": draw_slice_starts(jax.random.fold_in(arg_keys[3], 71), 0),
        "fine_ends": draw_fine_ends(jax.random.fold_in(arg_keys[3], 71), 0),
        "level_speeds": jnp.clip(jax.random.uniform(arg_keys[2], (2, NZ), jnp.float32, -0.15, 0.15), -0.15, 0.15),
    }


sound_speed = 0.15
diffusion = 0.08

def coarse_step(centre, east_side, west_side, level_speeds):
    north_side = jnp.roll(centre, -1, axis=2)
    south_side = jnp.roll(centre, 1, axis=2)
    diff_x = 0.5 * (east_side - west_side)
    diff_y = 0.5 * (north_side - south_side)
    laplace = east_side + west_side + north_side + south_side - 4.0 * centre
    advected = level_speeds[0] * diff_x + level_speeds[1] * diff_y - diffusion * laplace
    pressure = centre[0] - advected[0] - sound_speed * (diff_x[1] + diff_y[2])
    velocity_x = centre[1] - advected[1] - sound_speed * diff_x[0]
    velocity_y = centre[2] - advected[2] - sound_speed * diff_y[0]
    return jnp.stack([pressure, velocity_x, velocity_y])

def propagate(field_now, level_speeds):
    for _ in range(STEPS):
        field_now = coarse_step(field_now, jnp.roll(field_now, -1, axis=1), jnp.roll(field_now, 1, axis=1), level_speeds)
    return field_now

def cholesky_lower(matrix):
    highest = lax.Precision.HIGHEST
    order = matrix.shape[0]
    places = jnp.arange(order, dtype=jnp.int32)

    def column_step(column, factor):
        picked = (places == column).astype(matrix.dtype)
        factor_row = jnp.dot(picked, factor, precision=highest)
        target = jnp.dot(matrix, picked, precision=highest)
        remain = target - jnp.dot(factor, factor_row, precision=highest)
        pivot = jnp.sqrt(jnp.dot(remain, picked, precision=highest))
        below = jnp.where(places > column, remain / pivot, jnp.zeros_like(remain))
        fresh = jnp.where(places == column, pivot, below)
        return factor + fresh[:, None] * picked[None, :]
    return lax.fori_loop(0, order, column_step, jnp.zeros_like(matrix))

def lower_inverse(factor):
    highest = lax.Precision.HIGHEST
    order = factor.shape[0]
    places = jnp.arange(order, dtype=jnp.int32)

    def row_step(row, inverse):
        picked = (places == row).astype(factor.dtype)
        factor_row = jnp.dot(picked, factor, precision=highest)
        pivot = jnp.dot(factor_row, picked, precision=highest)
        earlier = jnp.where(places < row, factor_row, jnp.zeros_like(factor_row))
        fresh = (picked - jnp.dot(earlier, inverse, precision=highest)) / pivot
        return inverse + picked[:, None] * fresh[None, :]
    return lax.fori_loop(0, order, row_step, jnp.zeros_like(factor))

def reduced_chain(gram_total, cross_total, projected):
    highest = lax.Precision.HIGHEST
    lower_factor = cholesky_lower(gram_total)
    inverse_factor = lower_inverse(lower_factor)
    half_solve = jnp.dot(inverse_factor, cross_total, precision=highest)
    coarse_hat = jnp.dot(half_solve, inverse_factor.T, precision=highest)
    forcing = jnp.dot(inverse_factor, projected, precision=highest)

    def chain_link(coefficient, inputs):
        start_row, force_term = inputs
        change = jnp.dot(coarse_hat, coefficient - start_row, precision=highest)
        advanced = jnp.dot(coarse_hat, coefficient, precision=highest) + force_term
        return (advanced, change)
    last_coef, changes = lax.scan(chain_link, lower_factor[0], (lower_factor, forcing.T))
    shifted = jnp.concatenate([jnp.zeros_like(changes[:1]), changes[:-1]], axis=0)
    return jnp.dot(inverse_factor.T, shifted.T, precision=highest)

def reference(slice_starts, fine_ends, level_speeds):
    highest = lax.Precision.HIGHEST

    def one_slice(field_now):
        return propagate(field_now, level_speeds)
    coarse = lax.map(one_slice, slice_starts)
    fine_jumps = fine_ends - coarse
    flat_start = slice_starts.reshape(SLICES, -1)
    gram_total = jnp.dot(flat_start, flat_start.T, precision=highest)
    cross_total = jnp.dot(flat_start, coarse.reshape(SLICES, -1).T, precision=highest)
    projected = jnp.dot(flat_start, fine_jumps.reshape(SLICES, -1).T, precision=highest)
    weights = reduced_chain(gram_total, cross_total, projected)
    fresh_field = jnp.dot(weights.T, flat_start, precision=highest).reshape(slice_starts.shape)
    prior_state = jnp.concatenate([slice_starts[:1], fine_ends[:-1]], axis=0)
    return (prior_state + fresh_field, fine_jumps)
```

```python
import functools

import jax
import jax.numpy as jnp
from jax import lax
from jax.experimental import pallas as pl
from jax.experimental.pallas import tpu as pltpu
from jax.sharding import PartitionSpec as P

STEPS = 4
SOUND = 0.15
DIFFUSION = 0.08
HIGHEST = lax.Precision.HIGHEST
F32 = jnp.float32


def shaped(shape):
    return jax.ShapeDtypeStruct(shape, F32)


def cost(flops, nbytes):
    return pl.CostEstimate(flops=flops, bytes_accessed=nbytes, transcendentals=0)


def params():
    return pltpu.CompilerParams(vmem_limit_bytes=16 << 20)


def low_half():
    return lax.broadcasted_iota(jnp.int32, (16, 8, 128), 1) < 4


def to_chunks(first, second):
    one, two = first.reshape(16, 8, 128), second.reshape(16, 8, 128)
    low = low_half()
    even = jnp.where(low, one, pltpu.roll(two, 4, 1))
    odd = jnp.where(low, pltpu.roll(one, 4, 1), two)
    return even, odd


def from_chunks(even, odd):
    low = low_half()
    one = jnp.where(low, even, pltpu.roll(odd, 4, 1))
    two = jnp.where(low, pltpu.roll(even, 4, 1), odd)
    return one.reshape(128, 128), two.reshape(128, 128)


def chunk_kernel(tile_ref, out_ref):
    blocks = [
        tile_ref[field, 4 * part : 4 * part + 4].reshape(128, 128).T for field in range(3) for part in range(4)
    ]
    for pair in range(6):
        even, odd = to_chunks(blocks[2 * pair], blocks[2 * pair + 1])
        out_ref[:, 0, 8 * pair : 8 * pair + 8, :] = even
        out_ref[:, 1, 8 * pair : 8 * pair + 8, :] = odd


def chunked(tile):
    return pl.pallas_call(
        chunk_kernel, out_shape=shaped((16, 2, 48, 128)), name="chunked", cost_estimate=cost(0, 1600000), compiler_params=params()
    )(tile)


def unchunk_kernel(chunks_ref, out_ref):
    for pair in range(6):
        rows = slice(8 * pair, 8 * pair + 8)
        blocks = from_chunks(chunks_ref[:, 0, rows, :], chunks_ref[:, 1, rows, :])
        for half in range(2):
            field, part = divmod(2 * pair + half, 4)
            out_ref[field, 4 * part : 4 * part + 4] = blocks[half].T.reshape(4, 32, 128)


def unchunked(chunks):
    return pl.pallas_call(
        unchunk_kernel, out_shape=shaped((3, 16, 32, 128)), name="unchunked", cost_estimate=cost(0, 1600000), compiler_params=params()
    )(chunks)


def slab_kernel(chunks_ref, matrix_ref, slab_ref, first_ref, last_ref):
    for pair in range(6):
        rows = slice(8 * pair, 8 * pair + 8)
        blocks = from_chunks(chunks_ref[:, 0, rows, :], chunks_ref[:, 1, rows, :])
        for half in range(2):
            index = 2 * pair + half
            field, part = divmod(index, 4)
            matrix_ref[:, 128 * index : 128 * index + 128] = blocks[half]
            turned = blocks[half].T.reshape(4, 32, 128)
            slab_ref[field, 4 * part : 4 * part + 4] = turned
            if part == 0:
                first_ref[field] = turned
            if part == 3:
                last_ref[field] = turned


def slabbed(chunks):
    edge = (3, STEPS, 32, 128)
    return pl.pallas_call(
        slab_kernel,
        out_shape=(shaped((128, 1536)), shaped((3, 16, 32, 128)), shaped(edge), shaped(edge)),
        name="slabbed",
        cost_estimate=cost(0, 2800000), compiler_params=params(),
    )(chunks)


def advance(own_ref, before_ref, after_ref, speeds_ref, ping, pong):
    ping[:, 0:4] = before_ref[...]
    ping[:, 4:20] = own_ref[...]
    ping[:, 20:24] = after_ref[...]
    drift_x = 0.5 * speeds_ref[0:1, :]
    drift_y = 0.5 * speeds_ref[1:2, :]
    held, fresh = ping, pong
    for step in range(STEPS):

        def layer(place, _, held=held, fresh=fresh):
            centre, east, west = held[:, place], held[:, place + 1], held[:, place - 1]
            north = pltpu.roll(centre, 31, 1)
            south = pltpu.roll(centre, 1, 1)
            diff_x, diff_y = east - west, north - south
            around = (east + west) + (north + south)
            moved = (1.0 - 4.0 * DIFFUSION) * centre + DIFFUSION * around - drift_x * diff_x - drift_y * diff_y
            half = 0.5 * SOUND
            fresh[0, place] = moved[0] - half * (diff_x[1] + diff_y[2])
            fresh[1, place] = moved[1] - half * diff_x[0]
            fresh[2, place] = moved[2] - half * diff_y[0]
            return 0

        lax.fori_loop(step + 1, 23 - step, layer, 0)
        held, fresh = fresh, held
    return held


def jump_kernel(own_ref, before_ref, after_ref, speeds_ref, ends_ref, out_ref, ping, pong):
    coarse = advance(own_ref, before_ref, after_ref, speeds_ref, ping, pong)
    out_ref[...] = ends_ref[...] - coarse[:, 4:20]


def fine_jumps_of(own, before, after, speeds, ends):
    return pl.pallas_call(
        jump_kernel,
        out_shape=shaped((3, 16, 32, 128)),
        scratch_shapes=[pltpu.VMEM((3, 24, 32, 128), F32)] * 2,
        name="fine_jumps",
        cost_estimate=cost(18000000, 2800000), compiler_params=params(),
    )(own, before, after, speeds, ends)


def folded(product):
    row = lax.broadcasted_iota(jnp.int32, (128, 128), 0)
    lane = lax.broadcasted_iota(jnp.int32, (128, 128), 1)
    same = jnp.where((row & 3) == (lane & 3), product, 0.0)
    pick = spread()
    rows = jnp.dot(pick, same, precision=HIGHEST, preferred_element_type=F32)
    return lax.dot_general(rows, pick, (((1,), (1,)), ((), ())), precision=HIGHEST, preferred_element_type=F32)


def spread():
    row = lax.broadcasted_iota(jnp.int32, (32, 128), 0)
    lane = lax.broadcasted_iota(jnp.int32, (32, 128), 1)
    return jnp.where((lane >> 2) == row, 1.0, 0.0).astype(F32)


def packed(matrix):
    return jnp.concatenate([matrix[8 * part : 8 * part + 8] for part in range(4)], axis=1)


def unpacked(rows):
    return jnp.concatenate([rows[:, 32 * part : 32 * part + 32] for part in range(4)], axis=0)


def cross_kernel(own_ref, before_ref, after_ref, speeds_ref, matrix_ref, out_ref, ping, pong):
    coarse = advance(own_ref, before_ref, after_ref, speeds_ref, ping, pong)
    matrix = matrix_ref[...]
    gram = lax.dot_general(matrix, matrix, (((1,), (1,)), ((), ())), precision=HIGHEST, preferred_element_type=F32)
    cross = jnp.dot(matrix, coarse[:, 4:20].reshape(1536, 128), precision=HIGHEST, preferred_element_type=F32)
    out_ref[0:8] = packed(folded(gram))
    out_ref[8:16] = packed(folded(cross))


def gram_and_cross(own, before, after, speeds, matrix):
    return pl.pallas_call(
        cross_kernel,
        out_shape=shaped((16, 128)),
        scratch_shapes=[pltpu.VMEM((3, 24, 32, 128), F32)] * 2,
        name="gram_and_cross",
        cost_estimate=cost(18000000, 2800000), compiler_params=params(),
    )(own, before, after, speeds, matrix)


def ends_kernel(chunks_ref, starts_ref, pair_ref, ends_ref, out_ref):
    for pair in range(6):
        rows = slice(8 * pair, 8 * pair + 8)
        blocks = from_chunks(chunks_ref[:, 0, rows, :], chunks_ref[:, 1, rows, :])
        for half in range(2):
            index = 2 * pair + half
            ends_ref[:, 128 * index : 128 * index + 128] = blocks[half]
    product = lax.dot_general(
        starts_ref[...], ends_ref[...], (((1,), (1,)), ((), ())), precision=HIGHEST, preferred_element_type=F32
    )
    all_three = jnp.concatenate([pair_ref[...], packed(folded(product))], axis=0)
    out_ref[...] = jnp.broadcast_to(all_three[None], out_ref.shape)


def partial_sums(chunks, starts, pair, copies):
    return pl.pallas_call(
        ends_kernel,
        out_shape=(shaped((128, 1536)), shaped((copies, 24, 128))),
        name="partial_sums",
        cost_estimate=cost(50000000, 2800000), compiler_params=params(),
    )(chunks, starts, pair)


def total_kernel(parts_ref, out_ref):
    out_ref[...] = jnp.broadcast_to(jnp.sum(parts_ref[...], axis=0)[None], out_ref.shape)


def totals(parts, copies):
    return pl.pallas_call(
        total_kernel, out_shape=shaped((copies, 24, 128)), name="totals", cost_estimate=cost(100000, 600000), compiler_params=params()
    )(parts)


def weights_of(gram, cross, ends_cross):
    table = jnp.concatenate([gram, cross, ends_cross, jnp.zeros((32, 32), F32)], axis=1)
    row = lax.broadcasted_iota(jnp.int32, (32, 128), 0)
    lane = lax.broadcasted_iota(jnp.int32, (32, 128), 1)
    for place in range(32):
        pivot_row = table[place : place + 1] / table[place : place + 1, place : place + 1]
        column = jnp.where(row == place, 0.0, jnp.broadcast_to(table[:, place : place + 1], (32, 128)))
        kept = jnp.where(row == place, jnp.broadcast_to(pivot_row, (32, 128)), table)
        table = kept - column * pivot_row
    hat = table[:, 32:64]
    moved = jnp.concatenate([table[:, 64:96], jnp.zeros((32, 96), F32)], axis=1)
    change = pltpu.roll(moved, 1, 1) - jnp.where(row == lane, 1.0, 0.0)
    change = jnp.where((lane >= 1) & (lane < 32), change, 0.0)
    power = hat
    for level in range(5):
        reach = 1 << level
        shifted = jnp.where(lane >= reach, pltpu.roll(change, reach, 1), 0.0)
        change = change + jnp.dot(power, shifted, precision=HIGHEST, preferred_element_type=F32)
        if level < 4:
            power = jnp.dot(power, power, precision=HIGHEST, preferred_element_type=F32)
    before = jnp.where((lane >= 1) & (lane < 32), pltpu.roll(change, 1, 1), 0.0)
    return jnp.dot(hat, before, precision=HIGHEST, preferred_element_type=F32)[:, 0:32]


def fresh_kernel(parts_ref, starts_ref, ends_ref, out_ref):
    sums = jnp.sum(parts_ref[...], axis=0)
    weights = weights_of(unpacked(sums[0:8]), unpacked(sums[8:16]), unpacked(sums[16:24]))
    pick = spread()
    wide = jnp.dot(weights, pick, precision=HIGHEST, preferred_element_type=F32)
    whole = lax.dot_general(wide, pick, (((0,), (0,)), ((), ())), precision=HIGHEST, preferred_element_type=F32)
    row = lax.broadcasted_iota(jnp.int32, (128, 128), 0)
    lane = lax.broadcasted_iota(jnp.int32, (128, 128), 1)
    mixing = jnp.where((row & 3) == (lane & 3), whole, 0.0)
    for pair in range(6):
        blocks = []
        for half in range(2):
            columns = slice(256 * pair + 128 * half, 256 * pair + 128 * half + 128)
            starts = starts_ref[:, columns]
            prior = jnp.where(row < 4, starts, pltpu.roll(ends_ref[:, columns], 4, 0))
            blocks.append(prior + jnp.dot(mixing, starts, precision=HIGHEST, preferred_element_type=F32))
        even, odd = to_chunks(blocks[0], blocks[1])
        out_ref[:, 0, 8 * pair : 8 * pair + 8, :] = even
        out_ref[:, 1, 8 * pair : 8 * pair + 8, :] = odd


def fresh_chunks(parts, starts, ends):
    return pl.pallas_call(
        fresh_kernel,
        out_shape=shaped((16, 2, 48, 128)),
        name="fresh_chunks",
        cost_estimate=cost(50000000, 2800000), compiler_params=params(),
    )(parts, starts, ends)


def exchanged(chunks):
    moved = lax.all_to_all(chunks.reshape(32, 48, 128), "tm", split_axis=0, concat_axis=0, tiled=True)
    return moved.reshape(16, 2, 48, 128)


def sides(first, last):
    size = lax.axis_size("space")
    up = [(i, (i + 1) % size) for i in range(size)]
    down = [(j, i) for i, j in up]
    return lax.ppermute(last, "space", up), lax.ppermute(first, "space", down)


def on_device(slice_starts, fine_ends, level_speeds):
    space = lax.axis_size("space")
    starts, ends = slice_starts[0], fine_ends[0]
    levels = lax.dynamic_slice(level_speeds, (0, 4 * lax.axis_index("tm")), (2, 4))
    slab_speeds = jnp.tile(levels, (1, 32))
    start_chunks = exchanged(chunked(starts))
    end_chunks = exchanged(chunked(ends))
    before, after = sides(starts[:, :STEPS], starts[:, -STEPS:])
    fine_jumps = fine_jumps_of(starts, before, after, level_speeds, ends)
    matrix, slab, first, last = slabbed(start_chunks)
    slab_before, slab_after = sides(first, last)
    pair = gram_and_cross(slab, slab_before, slab_after, slab_speeds, matrix)
    end_matrix, parts = partial_sums(end_chunks, matrix, pair, space)
    parts = lax.all_to_all(parts, "space", split_axis=0, concat_axis=0, tiled=True)
    parts = totals(parts, 32)
    parts = lax.all_to_all(parts, "tm", split_axis=0, concat_axis=0, tiled=True)
    new_starts = unchunked(exchanged(fresh_chunks(parts, matrix, end_matrix)))
    return new_starts[None], fine_jumps[None]


def solution(mesh):
    in_specs = (P("tm", None, "space", None, None), P("tm", None, "space", None, None), P())
    out_specs = (P("tm", None, "space", None, None), P("tm", None, "space", None, None))
    return jax.shard_map(
        on_device, mesh=mesh, in_specs=in_specs, out_specs=out_specs, check_vma=False
    )
```

```python
import functools

import jax
import jax.numpy as jnp
from jax import lax
from jax.experimental import pallas as pl
from jax.experimental.pallas import tpu as pltpu
from jax.sharding import PartitionSpec as P

STEPS = 4
SOUND = 0.15
DIFFUSION = 0.08
HIGHEST = lax.Precision.HIGHEST
F32 = jnp.float32


def shaped(shape):
    return jax.ShapeDtypeStruct(shape, F32)


def cost(flops, nbytes):
    return pl.CostEstimate(flops=flops, bytes_accessed=nbytes, transcendentals=0)


def params():
    return pltpu.CompilerParams(vmem_limit_bytes=16 << 20)


def low_half():
    return lax.broadcasted_iota(jnp.int32, (16, 8, 128), 1) < 4


def to_chunks(first, second):
    one, two = first.reshape(16, 8, 128), second.reshape(16, 8, 128)
    low = low_half()
    even = jnp.where(low, one, pltpu.roll(two, 4, 1))
    odd = jnp.where(low, pltpu.roll(one, 4, 1), two)
    return even, odd


def from_chunks(even, odd):
    low = low_half()
    one = jnp.where(low, even, pltpu.roll(odd, 4, 1))
    two = jnp.where(low, pltpu.roll(even, 4, 1), odd)
    return one.reshape(128, 128), two.reshape(128, 128)


def chunk_kernel(tile_ref, out_ref):
    blocks = [
        tile_ref[field, 4 * part : 4 * part + 4].reshape(128, 128).T for field in range(3) for part in range(4)
    ]
    for pair in range(6):
        even, odd = to_chunks(blocks[2 * pair], blocks[2 * pair + 1])
        out_ref[:, 0, 8 * pair : 8 * pair + 8, :] = even
        out_ref[:, 1, 8 * pair : 8 * pair + 8, :] = odd


def chunked(tile):
    return pl.pallas_call(
        chunk_kernel, out_shape=shaped((16, 2, 48, 128)), name="chunked", cost_estimate=cost(0, 1600000), compiler_params=params()
    )(tile)


def unchunk_kernel(chunks_ref, out_ref):
    for pair in range(6):
        rows = slice(8 * pair, 8 * pair + 8)
        blocks = from_chunks(chunks_ref[:, 0, rows, :], chunks_ref[:, 1, rows, :])
        for half in range(2):
            field, part = divmod(2 * pair + half, 4)
            out_ref[field, 4 * part : 4 * part + 4] = blocks[half].T.reshape(4, 32, 128)


def unchunked(chunks):
    return pl.pallas_call(
        unchunk_kernel, out_shape=shaped((3, 16, 32, 128)), name="unchunked", cost_estimate=cost(0, 1600000), compiler_params=params()
    )(chunks)


def slab_kernel(chunks_ref, matrix_ref, slab_ref, first_ref, last_ref):
    for pair in range(6):
        rows = slice(8 * pair, 8 * pair + 8)
        blocks = from_chunks(chunks_ref[:, 0, rows, :], chunks_ref[:, 1, rows, :])
        for half in range(2):
            index = 2 * pair + half
            field, part = divmod(index, 4)
            matrix_ref[:, 128 * index : 128 * index + 128] = blocks[half]
            turned = blocks[half].T.reshape(4, 32, 128)
            slab_ref[field, 4 * part : 4 * part + 4] = turned
            if part == 0:
                first_ref[field] = turned
            if part == 3:
                last_ref[field] = turned


def slabbed(chunks):
    edge = (3, STEPS, 32, 128)
    return pl.pallas_call(
        slab_kernel,
        out_shape=(shaped((128, 1536)), shaped((3, 16, 32, 128)), shaped(edge), shaped(edge)),
        name="slabbed",
        cost_estimate=cost(0, 2800000), compiler_params=params(),
    )(chunks)


def advance(own_ref, before_ref, after_ref, speeds_ref, ping, pong):
    ping[:, 0:4] = before_ref[...]
    ping[:, 4:20] = own_ref[...]
    ping[:, 20:24] = after_ref[...]
    drift_x = 0.5 * speeds_ref[0:1, :]
    drift_y = 0.5 * speeds_ref[1:2, :]
    held, fresh = ping, pong
    for step in range(STEPS):

        def layer(place, _, held=held, fresh=fresh):
            centre, east, west = held[:, place], held[:, place + 1], held[:, place - 1]
            north = pltpu.roll(centre, 31, 1)
            south = pltpu.roll(centre, 1, 1)
            diff_x, diff_y = east - west, north - south
            around = (east + west) + (north + south)
            moved = (1.0 - 4.0 * DIFFUSION) * centre + DIFFUSION * around - drift_x * diff_x - drift_y * diff_y
            half = 0.5 * SOUND
            fresh[0, place] = moved[0] - half * (diff_x[1] + diff_y[2])
            fresh[1, place] = moved[1] - half * diff_x[0]
            fresh[2, place] = moved[2] - half * diff_y[0]
            return 0

        lax.fori_loop(step + 1, 23 - step, layer, 0)
        held, fresh = fresh, held
    return held


def jump_kernel(own_ref, before_ref, after_ref, speeds_ref, ends_ref, out_ref, ping, pong):
    coarse = advance(own_ref, before_ref, after_ref, speeds_ref, ping, pong)
    out_ref[...] = ends_ref[...] - coarse[:, 4:20]


def fine_jumps_of(own, before, after, speeds, ends):
    return pl.pallas_call(
        jump_kernel,
        out_shape=shaped((3, 16, 32, 128)),
        scratch_shapes=[pltpu.VMEM((3, 24, 32, 128), F32)] * 2,
        name="fine_jumps",
        cost_estimate=cost(18000000, 2800000), compiler_params=params(),
    )(own, before, after, speeds, ends)


def iota(rows, lanes, axis):
    return lax.broadcasted_iota(jnp.int32, (rows, lanes), axis)


def where_one(test):
    return jnp.where(test, 1.0, 0.0).astype(F32)


def multiply(left, right):
    return jnp.dot(left, right, precision=HIGHEST, preferred_element_type=F32)


def same_level():
    return (iota(128, 128, 0) & 3) == (iota(128, 128, 1) & 3)


def folded(product, place):
    pick = where_one((iota(32, 128, 1) >> 2) == iota(32, 128, 0))
    put = where_one((iota(128, 128, 0) >> 2) + 32 * place == iota(128, 128, 1))
    return multiply(multiply(pick, jnp.where(same_level(), product, 0.0)), put)


def packed(table):
    free = iota(8, 128, 1) >= 96
    return [
        jnp.where(free, pltpu.roll(table[24:32], 96 - 32 * part, 1), table[8 * part : 8 * part + 8])
        for part in range(3)
    ]


def unpacked(rows):
    group = iota(8, 128, 1) >> 5
    parts = [rows[8 * part : 8 * part + 8] for part in range(3)]
    moved = [pltpu.roll(parts[part], 32 + 32 * part, 1) for part in range(3)]
    last = jnp.where(group == 0, moved[0], jnp.where(group == 1, moved[1], moved[2]))
    return parts + [last]


def cross_kernel(own_ref, before_ref, after_ref, speeds_ref, matrix_ref, out_ref, ping, pong):
    coarse = advance(own_ref, before_ref, after_ref, speeds_ref, ping, pong)
    matrix = matrix_ref[...]
    gram = lax.dot_general(matrix, matrix, (((1,), (1,)), ((), ())), precision=HIGHEST, preferred_element_type=F32)
    cross = multiply(matrix, coarse[:, 4:20].reshape(1536, 128))
    out_ref[...] = folded(gram, 0) + folded(cross, 1)


def gram_and_cross(own, before, after, speeds, matrix):
    return pl.pallas_call(
        cross_kernel,
        out_shape=shaped((32, 128)),
        scratch_shapes=[pltpu.VMEM((3, 24, 32, 128), F32)] * 2,
        name="gram_and_cross",
        cost_estimate=cost(18000000, 2800000), compiler_params=params(),
    )(own, before, after, speeds, matrix)


def ends_kernel(chunks_ref, starts_ref, pair_ref, ends_ref, out_ref):
    for pair in range(6):
        rows = slice(8 * pair, 8 * pair + 8)
        blocks = from_chunks(chunks_ref[:, 0, rows, :], chunks_ref[:, 1, rows, :])
        for half in range(2):
            index = 2 * pair + half
            ends_ref[:, 128 * index : 128 * index + 128] = blocks[half]
    product = lax.dot_general(
        starts_ref[...], ends_ref[...], (((1,), (1,)), ((), ())), precision=HIGHEST, preferred_element_type=F32
    )
    parts = packed(pair_ref[...] + folded(product, 2))
    for part in range(3):
        out_ref[:, 8 * part : 8 * part + 8, :] = jnp.broadcast_to(parts[part][None], (out_ref.shape[0], 8, 128))


def partial_sums(chunks, starts, pair, copies):
    return pl.pallas_call(
        ends_kernel,
        out_shape=(shaped((128, 1536)), shaped((copies, 24, 128))),
        name="partial_sums",
        cost_estimate=cost(50000000, 2800000), compiler_params=params(),
    )(chunks, starts, pair)


def total_kernel(parts_ref, out_ref):
    out_ref[...] = jnp.broadcast_to(jnp.sum(parts_ref[...], axis=0)[None], out_ref.shape)


def totals(parts, copies):
    return pl.pallas_call(
        total_kernel, out_shape=shaped((copies, 24, 128)), name="totals", cost_estimate=cost(100000, 600000), compiler_params=params()
    )(parts)


def eliminated(blocks):
    row = iota(8, 128, 0)
    for panel in range(4):
        columns = [
            [jnp.broadcast_to(block[:, 8 * panel + q : 8 * panel + q + 1], (8, 128)) for block in blocks]
            for q in range(8)
        ]
        for m in range(8):
            is_pivot = row == m
            column = columns[m]
            scale = 1.0 / column[panel][m : m + 1]

            def reduced(target):
                pivot = jnp.broadcast_to(target[panel][m : m + 1] * scale, (8, 128))
                return [
                    jnp.where(is_pivot, pivot, block - column[place] * pivot)
                    if place == panel
                    else block - column[place] * pivot
                    for place, block in enumerate(target)
                ]

            for q in range(m + 1, 8):
                columns[q] = reduced(columns[q])
            blocks = reduced(blocks)
    return blocks


def mixing_of(blocks):
    turned = jnp.concatenate(eliminated(blocks), axis=0).T
    power, moved = turned[32:64], turned[64:96]
    wide = multiply(power, where_one((iota(32, 128, 1) >> 2) == iota(32, 128, 0)))
    slice_of = iota(128, 32, 0) >> 2
    unit = where_one((slice_of == iota(128, 32, 1)) & (slice_of >= 1))
    change = multiply(where_one(slice_of == iota(128, 32, 1) + 1), moved) - unit

    def later(value, rows):
        return jnp.concatenate([jnp.zeros((rows, 32), F32), value[: 128 - rows]], axis=0)

    for level in range(5):
        change = change + multiply(later(change, 4 << level), power)
        if level < 4:
            power = multiply(power, power)
    return jnp.where(same_level(), multiply(later(change, 4), wide), 0.0)


def fresh_kernel(parts_ref, starts_ref, ends_ref, out_ref, held, sems):
    mixing = mixing_of(unpacked(jnp.sum(parts_ref[...], axis=0)))
    first = iota(128, 256, 0) < 4
    copies = []
    for pair in range(6):
        columns = slice(256 * pair, 256 * pair + 256)
        starts = starts_ref[:, columns]
        prior = jnp.where(first, starts, pltpu.roll(ends_ref[:, columns], 4, 0))
        fresh = prior + multiply(mixing, starts)
        even, odd = to_chunks(fresh[:, 0:128], fresh[:, 128:256])
        rows = slice(8 * pair, 8 * pair + 8)
        held[:, 0, rows, :] = even
        held[:, 1, rows, :] = odd
        copy = pltpu.make_async_copy(held.at[:, :, rows], out_ref.at[:, :, rows], sems.at[pair])
        copy.start()
        copies.append(copy)
    for copy in copies:
        copy.wait()


def fresh_chunks(parts, starts, ends):
    return pl.pallas_call(
        fresh_kernel,
        out_shape=shaped((16, 2, 48, 128)),
        in_specs=[pl.BlockSpec(memory_space=pltpu.VMEM)] * 3,
        out_specs=pl.BlockSpec(memory_space=pl.ANY),
        scratch_shapes=[pltpu.VMEM((16, 2, 48, 128), F32), pltpu.SemaphoreType.DMA((6,))],
        name="fresh_chunks",
        cost_estimate=cost(50000000, 2800000), compiler_params=params(),
    )(parts, starts, ends)


def exchanged(chunks):
    moved = lax.all_to_all(chunks.reshape(32, 48, 128), "tm", split_axis=0, concat_axis=0, tiled=True)
    return moved.reshape(16, 2, 48, 128)


def sides(first, last):
    size = lax.axis_size("space")
    up = [(i, (i + 1) % size) for i in range(size)]
    down = [(j, i) for i, j in up]
    return lax.ppermute(last, "space", up), lax.ppermute(first, "space", down)


def on_device(slice_starts, fine_ends, level_speeds):
    space = lax.axis_size("space")
    starts, ends = slice_starts[0], fine_ends[0]
    levels = lax.dynamic_slice(level_speeds, (0, 4 * lax.axis_index("tm")), (2, 4))
    slab_speeds = jnp.tile(levels, (1, 32))
    start_chunks = exchanged(chunked(starts))
    end_chunks = exchanged(chunked(ends))
    before, after = sides(starts[:, :STEPS], starts[:, -STEPS:])
    fine_jumps = fine_jumps_of(starts, before, after, level_speeds, ends)
    matrix, slab, first, last = slabbed(start_chunks)
    slab_before, slab_after = sides(first, last)
    pair = gram_and_cross(slab, slab_before, slab_after, slab_speeds, matrix)
    end_matrix, parts = partial_sums(end_chunks, matrix, pair, space)
    parts = lax.all_to_all(parts, "space", split_axis=0, concat_axis=0, tiled=True)
    parts = totals(parts, 32)
    parts = lax.all_to_all(parts, "tm", split_axis=0, concat_axis=0, tiled=True)
    new_starts = unchunked(exchanged(fresh_chunks(parts, matrix, end_matrix)))
    return new_starts[None], fine_jumps[None]


def solution(mesh):
    in_specs = (P("tm", None, "space", None, None), P("tm", None, "space", None, None), P())
    out_specs = (P("tm", None, "space", None, None), P("tm", None, "space", None, None))
    return jax.shard_map(
        on_device, mesh=mesh, in_specs=in_specs, out_specs=out_specs, check_vma=False
    )
```

```python
import functools

import jax
import jax.numpy as jnp
from jax import lax
from jax.experimental import pallas as pl
from jax.experimental.pallas import tpu as pltpu
from jax.sharding import PartitionSpec as P

STEPS = 4
SOUND = 0.15
DIFFUSION = 0.08
HIGHEST = lax.Precision.HIGHEST
F32 = jnp.float32
PAUSE = 8000


def shaped(shape):
    return jax.ShapeDtypeStruct(shape, F32)


def cost(flops, nbytes):
    return pl.CostEstimate(flops=flops, bytes_accessed=nbytes, transcendentals=0)


def params():
    return pltpu.CompilerParams(vmem_limit_bytes=16 << 20)


def low_half():
    return lax.broadcasted_iota(jnp.int32, (16, 8, 128), 1) < 4


def to_chunks(first, second):
    one, two = first.reshape(16, 8, 128), second.reshape(16, 8, 128)
    low = low_half()
    even = jnp.where(low, one, pltpu.roll(two, 4, 1))
    odd = jnp.where(low, pltpu.roll(one, 4, 1), two)
    return even, odd


def from_chunks(even, odd):
    low = low_half()
    one = jnp.where(low, even, pltpu.roll(odd, 4, 1))
    two = jnp.where(low, pltpu.roll(even, 4, 1), odd)
    return one.reshape(128, 128), two.reshape(128, 128)


def chunk_kernel(pause, tile_ref, out_ref):
    if pause:

        @pl.when(lax.rem(lax.axis_index("space"), 2) == 1)
        def _():
            pl.delay(pause)

    blocks = [
        tile_ref[field, 4 * part : 4 * part + 4].reshape(128, 128).T for field in range(3) for part in range(4)
    ]
    for pair in range(6):
        even, odd = to_chunks(blocks[2 * pair], blocks[2 * pair + 1])
        out_ref[:, 0, 8 * pair : 8 * pair + 8, :] = even
        out_ref[:, 1, 8 * pair : 8 * pair + 8, :] = odd


def chunked(tile, pause=0):
    return pl.pallas_call(
        functools.partial(chunk_kernel, pause), out_shape=shaped((16, 2, 48, 128)), name="chunked", cost_estimate=cost(0, 1600000), compiler_params=params()
    )(tile)


def unchunk_kernel(chunks_ref, out_ref):
    for pair in range(6):
        rows = slice(8 * pair, 8 * pair + 8)
        blocks = from_chunks(chunks_ref[:, 0, rows, :], chunks_ref[:, 1, rows, :])
        for half in range(2):
            field, part = divmod(2 * pair + half, 4)
            out_ref[field, 4 * part : 4 * part + 4] = blocks[half].T.reshape(4, 32, 128)


def unchunked(chunks):
    return pl.pallas_call(
        unchunk_kernel, out_shape=shaped((3, 16, 32, 128)), name="unchunked", cost_estimate=cost(0, 1600000), compiler_params=params()
    )(chunks)


def slab_kernel(chunks_ref, matrix_ref, slab_ref, first_ref, last_ref):
    for pair in range(6):
        rows = slice(8 * pair, 8 * pair + 8)
        blocks = from_chunks(chunks_ref[:, 0, rows, :], chunks_ref[:, 1, rows, :])
        for half in range(2):
            index = 2 * pair + half
            field, part = divmod(index, 4)
            matrix_ref[:, 128 * index : 128 * index + 128] = blocks[half]
            turned = blocks[half].T.reshape(4, 32, 128)
            slab_ref[field, 4 * part : 4 * part + 4] = turned
            if part == 0:
                first_ref[field] = turned
            if part == 3:
                last_ref[field] = turned


def slabbed(chunks):
    edge = (3, STEPS, 32, 128)
    return pl.pallas_call(
        slab_kernel,
        out_shape=(shaped((128, 1536)), shaped((3, 16, 32, 128)), shaped(edge), shaped(edge)),
        name="slabbed",
        cost_estimate=cost(0, 2800000), compiler_params=params(),
    )(chunks)


def advance(own_ref, before_ref, after_ref, speeds_ref, ping, pong):
    ping[:, 0:4] = before_ref[...]
    ping[:, 4:20] = own_ref[...]
    ping[:, 20:24] = after_ref[...]
    drift_x = 0.5 * speeds_ref[0:1, :]
    drift_y = 0.5 * speeds_ref[1:2, :]
    held, fresh = ping, pong
    for step in range(STEPS):

        def layer(place, _, held=held, fresh=fresh):
            centre, east, west = held[:, place], held[:, place + 1], held[:, place - 1]
            north = pltpu.roll(centre, 31, 1)
            south = pltpu.roll(centre, 1, 1)
            diff_x, diff_y = east - west, north - south
            around = (east + west) + (north + south)
            moved = (1.0 - 4.0 * DIFFUSION) * centre + DIFFUSION * around - drift_x * diff_x - drift_y * diff_y
            half = 0.5 * SOUND
            fresh[0, place] = moved[0] - half * (diff_x[1] + diff_y[2])
            fresh[1, place] = moved[1] - half * diff_x[0]
            fresh[2, place] = moved[2] - half * diff_y[0]
            return 0

        lax.fori_loop(step + 1, 23 - step, layer, 0)
        held, fresh = fresh, held
    return held


def jump_kernel(own_ref, before_ref, after_ref, speeds_ref, ends_ref, out_ref, ping, pong):
    coarse = advance(own_ref, before_ref, after_ref, speeds_ref, ping, pong)
    out_ref[...] = ends_ref[...] - coarse[:, 4:20]


def fine_jumps_of(own, before, after, speeds, ends):
    return pl.pallas_call(
        jump_kernel,
        out_shape=shaped((3, 16, 32, 128)),
        scratch_shapes=[pltpu.VMEM((3, 24, 32, 128), F32)] * 2,
        name="fine_jumps",
        cost_estimate=cost(18000000, 2800000), compiler_params=params(),
    )(own, before, after, speeds, ends)


def iota(rows, lanes, axis):
    return lax.broadcasted_iota(jnp.int32, (rows, lanes), axis)


def where_one(test):
    return jnp.where(test, 1.0, 0.0).astype(F32)


def multiply(left, right):
    return jnp.dot(left, right, precision=HIGHEST, preferred_element_type=F32)


def same_level():
    return (iota(128, 128, 0) & 3) == (iota(128, 128, 1) & 3)


def folded(product, place):
    pick = where_one((iota(32, 128, 1) >> 2) == iota(32, 128, 0))
    put = where_one((iota(128, 128, 0) >> 2) + 32 * place == iota(128, 128, 1))
    return multiply(multiply(pick, jnp.where(same_level(), product, 0.0)), put)


def packed(table):
    free = iota(8, 128, 1) >= 96
    return [
        jnp.where(free, pltpu.roll(table[24:32], 96 - 32 * part, 1), table[8 * part : 8 * part + 8])
        for part in range(3)
    ]


def unpacked(rows):
    group = iota(8, 128, 1) >> 5
    parts = [rows[8 * part : 8 * part + 8] for part in range(3)]
    moved = [pltpu.roll(parts[part], 32 + 32 * part, 1) for part in range(3)]
    last = jnp.where(group == 0, moved[0], jnp.where(group == 1, moved[1], moved[2]))
    return parts + [last]


def cross_kernel(own_ref, before_ref, after_ref, speeds_ref, matrix_ref, out_ref, ping, pong):
    coarse = advance(own_ref, before_ref, after_ref, speeds_ref, ping, pong)
    matrix = matrix_ref[...]
    gram = lax.dot_general(matrix, matrix, (((1,), (1,)), ((), ())), precision=HIGHEST, preferred_element_type=F32)
    cross = multiply(matrix, coarse[:, 4:20].reshape(1536, 128))
    out_ref[...] = folded(gram, 0) + folded(cross, 1)


def gram_and_cross(own, before, after, speeds, matrix):
    return pl.pallas_call(
        cross_kernel,
        out_shape=shaped((32, 128)),
        scratch_shapes=[pltpu.VMEM((3, 24, 32, 128), F32)] * 2,
        name="gram_and_cross",
        cost_estimate=cost(18000000, 2800000), compiler_params=params(),
    )(own, before, after, speeds, matrix)


def ends_kernel(chunks_ref, starts_ref, pair_ref, ends_ref, out_ref):
    for pair in range(6):
        rows = slice(8 * pair, 8 * pair + 8)
        blocks = from_chunks(chunks_ref[:, 0, rows, :], chunks_ref[:, 1, rows, :])
        for half in range(2):
            index = 2 * pair + half
            ends_ref[:, 128 * index : 128 * index + 128] = blocks[half]
    product = lax.dot_general(
        starts_ref[...], ends_ref[...], (((1,), (1,)), ((), ())), precision=HIGHEST, preferred_element_type=F32
    )
    parts = packed(pair_ref[...] + folded(product, 2))
    for part in range(3):
        out_ref[:, 8 * part : 8 * part + 8, :] = jnp.broadcast_to(parts[part][None], (out_ref.shape[0], 8, 128))


def partial_sums(chunks, starts, pair, copies):
    return pl.pallas_call(
        ends_kernel,
        out_shape=(shaped((128, 1536)), shaped((copies, 24, 128))),
        name="partial_sums",
        cost_estimate=cost(50000000, 2800000), compiler_params=params(),
    )(chunks, starts, pair)


def total_kernel(parts_ref, out_ref):
    out_ref[...] = jnp.broadcast_to(jnp.sum(parts_ref[...], axis=0)[None], out_ref.shape)


def totals(parts, copies):
    return pl.pallas_call(
        total_kernel, out_shape=shaped((copies, 24, 128)), name="totals", cost_estimate=cost(100000, 600000), compiler_params=params()
    )(parts)


def eliminated(blocks):
    row = iota(8, 128, 0)
    for panel in range(4):
        columns = [
            [jnp.broadcast_to(block[:, 8 * panel + q : 8 * panel + q + 1], (8, 128)) for block in blocks]
            for q in range(8)
        ]
        for m in range(8):
            is_pivot = row == m
            column = columns[m]
            scale = 1.0 / column[panel][m : m + 1]

            def reduced(target):
                pivot = jnp.broadcast_to(target[panel][m : m + 1] * scale, (8, 128))
                return [
                    jnp.where(is_pivot, pivot, block - column[place] * pivot)
                    if place == panel
                    else block - column[place] * pivot
                    for place, block in enumerate(target)
                ]

            for q in range(m + 1, 8):
                columns[q] = reduced(columns[q])
            blocks = reduced(blocks)
    return blocks


def mixing_of(blocks):
    turned = jnp.concatenate(eliminated(blocks), axis=0).T
    power, moved = turned[32:64], turned[64:96]
    wide = multiply(power, where_one((iota(32, 128, 1) >> 2) == iota(32, 128, 0)))
    slice_of = iota(128, 32, 0) >> 2
    unit = where_one((slice_of == iota(128, 32, 1)) & (slice_of >= 1))
    change = multiply(where_one(slice_of == iota(128, 32, 1) + 1), moved) - unit

    def later(value, rows):
        return jnp.concatenate([jnp.zeros((rows, 32), F32), value[: 128 - rows]], axis=0)

    for level in range(5):
        change = change + multiply(later(change, 4 << level), power)
        if level < 4:
            power = multiply(power, power)
    return jnp.where(same_level(), multiply(later(change, 4), wide), 0.0)


def fresh_kernel(parts_ref, starts_ref, ends_ref, out_ref, held, sems):
    mixing = mixing_of(unpacked(jnp.sum(parts_ref[...], axis=0)))
    first = iota(128, 256, 0) < 4
    copies = []
    for pair in range(6):
        columns = slice(256 * pair, 256 * pair + 256)
        starts = starts_ref[:, columns]
        prior = jnp.where(first, starts, pltpu.roll(ends_ref[:, columns], 4, 0))
        fresh = prior + multiply(mixing, starts)
        even, odd = to_chunks(fresh[:, 0:128], fresh[:, 128:256])
        rows = slice(8 * pair, 8 * pair + 8)
        held[:, 0, rows, :] = even
        held[:, 1, rows, :] = odd
        copy = pltpu.make_async_copy(held.at[:, :, rows], out_ref.at[:, :, rows], sems.at[pair])
        copy.start()
        copies.append(copy)
    for copy in copies:
        copy.wait()


def fresh_chunks(parts, starts, ends):
    return pl.pallas_call(
        fresh_kernel,
        out_shape=shaped((16, 2, 48, 128)),
        in_specs=[pl.BlockSpec(memory_space=pltpu.VMEM)] * 3,
        out_specs=pl.BlockSpec(memory_space=pl.ANY),
        scratch_shapes=[pltpu.VMEM((16, 2, 48, 128), F32), pltpu.SemaphoreType.DMA((6,))],
        name="fresh_chunks",
        cost_estimate=cost(50000000, 2800000), compiler_params=params(),
    )(parts, starts, ends)


def exchanged(chunks):
    moved = lax.all_to_all(chunks.reshape(32, 48, 128), "tm", split_axis=0, concat_axis=0, tiled=True)
    return moved.reshape(16, 2, 48, 128)


def sides(first, last):
    size = lax.axis_size("space")
    up = [(i, (i + 1) % size) for i in range(size)]
    down = [(j, i) for i, j in up]
    return lax.ppermute(last, "space", up), lax.ppermute(first, "space", down)


def on_device(slice_starts, fine_ends, level_speeds):
    space = lax.axis_size("space")
    starts, ends = slice_starts[0], fine_ends[0]
    levels = lax.dynamic_slice(level_speeds, (0, 4 * lax.axis_index("tm")), (2, 4))
    slab_speeds = jnp.tile(levels, (1, 32))
    start_chunks = exchanged(chunked(starts, PAUSE))
    end_chunks = exchanged(chunked(ends))
    before, after = sides(starts[:, :STEPS], starts[:, -STEPS:])
    fine_jumps = fine_jumps_of(starts, before, after, level_speeds, ends)
    matrix, slab, first, last = slabbed(start_chunks)
    slab_before, slab_after = sides(first, last)
    pair = gram_and_cross(slab, slab_before, slab_after, slab_speeds, matrix)
    end_matrix, parts = partial_sums(end_chunks, matrix, pair, space)
    parts = lax.all_to_all(parts, "space", split_axis=0, concat_axis=0, tiled=True)
    parts = totals(parts, 32)
    parts = lax.all_to_all(parts, "tm", split_axis=0, concat_axis=0, tiled=True)
    new_starts = unchunked(exchanged(fresh_chunks(parts, matrix, end_matrix)))
    return new_starts[None], fine_jumps[None]


def solution(mesh):
    in_specs = (P("tm", None, "space", None, None), P("tm", None, "space", None, None), P())
    out_specs = (P("tm", None, "space", None, None), P("tm", None, "space", None, None))
    return jax.shard_map(
        on_device, mesh=mesh, in_specs=in_specs, out_specs=out_specs, check_vma=False
    )
```

```python
import functools

import jax
import jax.numpy as jnp
from jax import lax
from jax.experimental import pallas as pl
from jax.experimental.pallas import tpu as pltpu
from jax.sharding import PartitionSpec as P

STEPS = 4
SOUND = 0.15
DIFFUSION = 0.08
HIGHEST = lax.Precision.HIGHEST
F32 = jnp.float32
PAUSE = 8000


def shaped(shape):
    return jax.ShapeDtypeStruct(shape, F32)


def cost(flops, nbytes):
    return pl.CostEstimate(flops=flops, bytes_accessed=nbytes, transcendentals=0)


def params(limit=16 << 20):
    return pltpu.CompilerParams(vmem_limit_bytes=limit)


def low_half():
    return lax.broadcasted_iota(jnp.int32, (16, 8, 128), 1) < 4


def to_chunks(first, second):
    one, two = first.reshape(16, 8, 128), second.reshape(16, 8, 128)
    low = low_half()
    even = jnp.where(low, one, pltpu.roll(two, 4, 1))
    odd = jnp.where(low, pltpu.roll(one, 4, 1), two)
    return even, odd


def from_chunks(even, odd):
    low = low_half()
    one = jnp.where(low, even, pltpu.roll(odd, 4, 1))
    two = jnp.where(low, pltpu.roll(even, 4, 1), odd)
    return one.reshape(128, 128), two.reshape(128, 128)


def chunk_kernel(pause, tile_ref, out_ref, tile, held, in_sems, out_sems):
    arriving = [pltpu.make_async_copy(tile_ref.at[field], tile.at[field], in_sems.at[field]) for field in range(3)]
    for copy in arriving:
        copy.start()
    if pause:

        @pl.when(lax.rem(lax.axis_index("space"), 2) == 0)
        def _():
            pl.delay(pause)

    leaving = []
    for pair in range(6):
        if pair % 2 == 0:
            arriving[pair // 2].wait()
        blocks = []
        for half in range(2):
            field, part = divmod(2 * pair + half, 4)
            blocks.append(tile[field, 4 * part : 4 * part + 4].reshape(128, 128).T)
        rows = slice(8 * pair, 8 * pair + 8)
        even, odd = to_chunks(blocks[0], blocks[1])
        held[:, 0, rows, :] = even
        held[:, 1, rows, :] = odd
        copy = pltpu.make_async_copy(held.at[:, :, rows], out_ref.at[:, :, rows], out_sems.at[pair])
        copy.start()
        leaving.append(copy)
    for copy in leaving:
        copy.wait()


def chunked(tile, pause=0):
    return pl.pallas_call(
        functools.partial(chunk_kernel, pause),
        out_shape=shaped((16, 2, 48, 128)),
        in_specs=[pl.BlockSpec(memory_space=pltpu.HBM)],
        out_specs=pl.BlockSpec(memory_space=pltpu.HBM),
        scratch_shapes=[
            pltpu.VMEM((3, 16, 32, 128), F32),
            pltpu.VMEM((16, 2, 48, 128), F32),
            pltpu.SemaphoreType.DMA((3,)),
            pltpu.SemaphoreType.DMA((6,)),
        ],
        name="chunked",
        cost_estimate=cost(0, 1600000),
        compiler_params=params(67000000) if pause else params(),
    )(tile)


def unchunk_kernel(chunks_ref, out_ref, held, sems):
    leaving = []
    for pair in range(6):
        rows = slice(8 * pair, 8 * pair + 8)
        blocks = from_chunks(chunks_ref[:, 0, rows, :], chunks_ref[:, 1, rows, :])
        field, part = divmod(2 * pair, 4)
        for half in range(2):
            layer = 4 * (part + half)
            held[field, layer : layer + 4] = blocks[half].T.reshape(4, 32, 128)
        layers = slice(4 * part, 4 * part + 8)
        copy = pltpu.make_async_copy(held.at[field, layers], out_ref.at[field, layers], sems.at[pair])
        copy.start()
        leaving.append(copy)
    for copy in leaving:
        copy.wait()


def unchunked(chunks):
    return pl.pallas_call(
        unchunk_kernel,
        out_shape=shaped((3, 16, 32, 128)),
        in_specs=[pl.BlockSpec(memory_space=pltpu.VMEM)],
        out_specs=pl.BlockSpec(memory_space=pltpu.HBM),
        scratch_shapes=[pltpu.VMEM((3, 16, 32, 128), F32), pltpu.SemaphoreType.DMA((6,))],
        name="unchunked",
        cost_estimate=cost(0, 1600000),
        compiler_params=params(),
    )(chunks)


def slab_kernel(chunks_ref, matrix_ref, slab_ref, first_ref, last_ref):
    for pair in range(6):
        rows = slice(8 * pair, 8 * pair + 8)
        blocks = from_chunks(chunks_ref[:, 0, rows, :], chunks_ref[:, 1, rows, :])
        for half in range(2):
            index = 2 * pair + half
            field, part = divmod(index, 4)
            matrix_ref[:, 128 * index : 128 * index + 128] = blocks[half]
            turned = blocks[half].T.reshape(4, 32, 128)
            slab_ref[field, 4 * part : 4 * part + 4] = turned
            if part == 0:
                first_ref[field] = turned
            if part == 3:
                last_ref[field] = turned


def slabbed(chunks):
    edge = (3, STEPS, 32, 128)
    return pl.pallas_call(
        slab_kernel,
        out_shape=(shaped((128, 1536)), shaped((3, 16, 32, 128)), shaped(edge), shaped(edge)),
        name="slabbed",
        cost_estimate=cost(0, 2800000), compiler_params=params(),
    )(chunks)


def advance(own_ref, before_ref, after_ref, speeds_ref, ping, pong):
    ping[:, 0:4] = before_ref[...]
    ping[:, 4:20] = own_ref[...]
    ping[:, 20:24] = after_ref[...]
    drift_x = 0.5 * speeds_ref[0:1, :]
    drift_y = 0.5 * speeds_ref[1:2, :]
    held, fresh = ping, pong
    for step in range(STEPS):

        def layer(place, _, held=held, fresh=fresh):
            centre, east, west = held[:, place], held[:, place + 1], held[:, place - 1]
            north = pltpu.roll(centre, 31, 1)
            south = pltpu.roll(centre, 1, 1)
            diff_x, diff_y = east - west, north - south
            around = (east + west) + (north + south)
            moved = (1.0 - 4.0 * DIFFUSION) * centre + DIFFUSION * around - drift_x * diff_x - drift_y * diff_y
            half = 0.5 * SOUND
            fresh[0, place] = moved[0] - half * (diff_x[1] + diff_y[2])
            fresh[1, place] = moved[1] - half * diff_x[0]
            fresh[2, place] = moved[2] - half * diff_y[0]
            return 0

        lax.fori_loop(step + 1, 23 - step, layer, 0)
        held, fresh = fresh, held
    return held


def jump_kernel(own_ref, before_ref, after_ref, speeds_ref, ends_ref, out_ref, ping, pong):
    coarse = advance(own_ref, before_ref, after_ref, speeds_ref, ping, pong)
    out_ref[...] = ends_ref[...] - coarse[:, 4:20]


def fine_jumps_of(own, before, after, speeds, ends):
    return pl.pallas_call(
        jump_kernel,
        out_shape=shaped((3, 16, 32, 128)),
        scratch_shapes=[pltpu.VMEM((3, 24, 32, 128), F32)] * 2,
        name="fine_jumps",
        cost_estimate=cost(18000000, 2800000), compiler_params=params(),
    )(own, before, after, speeds, ends)


def iota(rows, lanes, axis):
    return lax.broadcasted_iota(jnp.int32, (rows, lanes), axis)


def where_one(test):
    return jnp.where(test, 1.0, 0.0).astype(F32)


def multiply(left, right):
    return jnp.dot(left, right, precision=HIGHEST, preferred_element_type=F32)


def pieces(value):
    first = value.astype(jnp.bfloat16)
    left = value - first.astype(F32)
    second = left.astype(jnp.bfloat16)
    third = (left - second.astype(F32)).astype(jnp.bfloat16)
    return first, second, third


def same_level():
    return (iota(128, 128, 0) & 3) == (iota(128, 128, 1) & 3)


def folded(product, place):
    pick = where_one((iota(32, 128, 1) >> 2) == iota(32, 128, 0))
    put = where_one((iota(128, 128, 0) >> 2) + 32 * place == iota(128, 128, 1))
    return multiply(multiply(pick, jnp.where(same_level(), product, 0.0)), put)


def packed(table):
    free = iota(8, 128, 1) >= 96
    return [
        jnp.where(free, pltpu.roll(table[24:32], 96 - 32 * part, 1), table[8 * part : 8 * part + 8])
        for part in range(3)
    ]


def unpacked(rows):
    group = iota(8, 128, 1) >> 5
    parts = [rows[8 * part : 8 * part + 8] for part in range(3)]
    moved = [pltpu.roll(parts[part], 32 + 32 * part, 1) for part in range(3)]
    last = jnp.where(group == 0, moved[0], jnp.where(group == 1, moved[1], moved[2]))
    return parts + [last]


def cross_kernel(own_ref, before_ref, after_ref, speeds_ref, matrix_ref, out_ref, pieces_ref, ping, pong):
    for index in range(12):
        lanes = slice(128 * index, 128 * index + 128)
        for place, piece in enumerate(pieces(matrix_ref[:, lanes])):
            pieces_ref[128 * place : 128 * place + 128, lanes] = piece
    coarse = advance(own_ref, before_ref, after_ref, speeds_ref, ping, pong)
    matrix = matrix_ref[...]
    gram = lax.dot_general(matrix, matrix, (((1,), (1,)), ((), ())), precision=HIGHEST, preferred_element_type=F32)
    cross = multiply(matrix, coarse[:, 4:20].reshape(1536, 128))
    out_ref[...] = folded(gram, 0) + folded(cross, 1)


def gram_and_cross(own, before, after, speeds, matrix):
    return pl.pallas_call(
        cross_kernel,
        out_shape=(shaped((32, 128)), jax.ShapeDtypeStruct((384, 1536), jnp.bfloat16)),
        scratch_shapes=[pltpu.VMEM((3, 24, 32, 128), F32)] * 2,
        name="gram_and_cross",
        cost_estimate=cost(18000000, 2800000), compiler_params=params(),
    )(own, before, after, speeds, matrix)


def ends_kernel(chunks_ref, starts_ref, pair_ref, ends_ref, out_ref, split):
    for pair in range(6):
        rows = slice(8 * pair, 8 * pair + 8)
        blocks = from_chunks(chunks_ref[:, 0, rows, :], chunks_ref[:, 1, rows, :])
        for half in range(2):
            index = 2 * pair + half
            lanes = slice(128 * index, 128 * index + 128)
            ends_ref[:, lanes] = blocks[half]
            for place, piece in enumerate(pieces(blocks[half])):
                split[128 * place : 128 * place + 128, lanes] = piece

    def against(rows, columns):
        return lax.dot_general(
            starts_ref[0:rows], split[columns], (((1,), (1,)), ((), ())), preferred_element_type=F32
        )

    low, high = against(384, slice(0, 256)), against(128, slice(256, 384))
    product = (low[256:384, 0:128] + low[128:256, 128:256] + high) + (low[128:256, 0:128] + low[0:128, 128:256])
    product = product + low[0:128, 0:128]
    parts = packed(pair_ref[...] + folded(product, 2))
    for part in range(3):
        out_ref[:, 8 * part : 8 * part + 8, :] = jnp.broadcast_to(parts[part][None], (out_ref.shape[0], 8, 128))


def partial_sums(chunks, starts, pair, copies):
    return pl.pallas_call(
        ends_kernel,
        out_shape=(shaped((128, 1536)), shaped((copies, 24, 128))),
        scratch_shapes=[pltpu.VMEM((384, 1536), jnp.bfloat16)],
        name="partial_sums",
        cost_estimate=cost(50000000, 2800000), compiler_params=params(),
    )(chunks, starts, pair)


def total_kernel(parts_ref, out_ref):
    out_ref[...] = jnp.broadcast_to(jnp.sum(parts_ref[...], axis=0)[None], out_ref.shape)


def totals(parts, copies):
    return pl.pallas_call(
        total_kernel, out_shape=shaped((copies, 24, 128)), name="totals", cost_estimate=cost(100000, 600000), compiler_params=params()
    )(parts)


def eliminated(blocks):
    row = iota(8, 128, 0)
    for panel in range(4):
        columns = [
            [jnp.broadcast_to(block[:, 8 * panel + q : 8 * panel + q + 1], (8, 128)) for block in blocks]
            for q in range(8)
        ]
        for m in range(8):
            is_pivot = row == m
            column = columns[m]
            scale = 1.0 / column[panel][m : m + 1]

            def reduced(target):
                pivot = jnp.broadcast_to(target[panel][m : m + 1] * scale, (8, 128))
                return [
                    jnp.where(is_pivot, pivot, block - column[place] * pivot)
                    if place == panel
                    else block - column[place] * pivot
                    for place, block in enumerate(target)
                ]

            for q in range(m + 1, 8):
                columns[q] = reduced(columns[q])
            blocks = reduced(blocks)
    return blocks


def mixing_of(blocks):
    turned = jnp.concatenate(eliminated(blocks), axis=0).T
    power, moved = turned[32:64], turned[64:96]
    wide = multiply(power, where_one((iota(32, 128, 1) >> 2) == iota(32, 128, 0)))
    slice_of = iota(128, 32, 0) >> 2
    unit = where_one((slice_of == iota(128, 32, 1)) & (slice_of >= 1))
    change = multiply(where_one(slice_of == iota(128, 32, 1) + 1), moved) - unit

    def later(value, rows):
        return jnp.concatenate([jnp.zeros((rows, 32), F32), value[: 128 - rows]], axis=0)

    for level in range(5):
        change = change + multiply(later(change, 4 << level), power)
        if level < 4:
            power = multiply(power, power)
    return jnp.where(same_level(), multiply(later(change, 4), wide), 0.0)


def fresh_kernel(parts_ref, starts_ref, pieces_ref, ends_ref, out_ref, held, sems):
    one, two, three = pieces(mixing_of(unpacked(jnp.sum(parts_ref[...], axis=0))))
    mixing = jnp.concatenate([three, two, one, two, one, one], axis=1)
    first = iota(128, 256, 0) < 4
    copies = []
    for pair in range(6):
        columns = slice(256 * pair, 256 * pair + 256)
        starts = starts_ref[:, columns]
        prior = jnp.where(first, starts, pltpu.roll(ends_ref[:, columns], 4, 0))
        split = [pieces_ref[128 * place : 128 * place + 128, columns] for place in range(3)]
        split = jnp.concatenate([split[0], split[1], split[2], split[0], split[1], split[0]], axis=0)
        fresh = prior + jnp.dot(mixing, split, preferred_element_type=F32)
        even, odd = to_chunks(fresh[:, 0:128], fresh[:, 128:256])
        rows = slice(8 * pair, 8 * pair + 8)
        held[:, 0, rows, :] = even
        held[:, 1, rows, :] = odd
        copy = pltpu.make_async_copy(held.at[:, :, rows], out_ref.at[:, :, rows], sems.at[pair])
        copy.start()
        copies.append(copy)
    for copy in copies:
        copy.wait()


def fresh_chunks(parts, starts, split, ends):
    return pl.pallas_call(
        fresh_kernel,
        out_shape=shaped((16, 2, 48, 128)),
        in_specs=[pl.BlockSpec(memory_space=pltpu.VMEM)] * 4,
        out_specs=pl.BlockSpec(memory_space=pl.ANY),
        scratch_shapes=[pltpu.VMEM((16, 2, 48, 128), F32), pltpu.SemaphoreType.DMA((6,))],
        name="fresh_chunks",
        cost_estimate=cost(50000000, 2800000), compiler_params=params(),
    )(parts, starts, split, ends)


def exchanged(chunks):
    moved = lax.all_to_all(chunks.reshape(32, 48, 128), "tm", split_axis=0, concat_axis=0, tiled=True)
    return moved.reshape(16, 2, 48, 128)


def sides(first, last):
    size = lax.axis_size("space")
    up = [(i, (i + 1) % size) for i in range(size)]
    down = [(j, i) for i, j in up]
    return lax.ppermute(last, "space", up), lax.ppermute(first, "space", down)


def on_device(slice_starts, fine_ends, level_speeds):
    space = lax.axis_size("space")
    starts, ends = slice_starts[0], fine_ends[0]
    levels = lax.dynamic_slice(level_speeds, (0, 4 * lax.axis_index("tm")), (2, 4))
    slab_speeds = jnp.tile(levels, (1, 32))
    start_chunks = exchanged(chunked(starts, PAUSE))
    end_chunks = exchanged(chunked(ends))
    before, after = sides(starts[:, :STEPS], starts[:, -STEPS:])
    fine_jumps = fine_jumps_of(starts, before, after, level_speeds, ends)
    matrix, slab, first, last = slabbed(start_chunks)
    slab_before, slab_after = sides(first, last)
    pair, split = gram_and_cross(slab, slab_before, slab_after, slab_speeds, matrix)
    end_matrix, parts = partial_sums(end_chunks, split, pair, space)
    parts = lax.all_to_all(parts, "space", split_axis=0, concat_axis=0, tiled=True)
    parts = totals(parts, 32)
    parts = lax.all_to_all(parts, "tm", split_axis=0, concat_axis=0, tiled=True)
    new_starts = unchunked(exchanged(fresh_chunks(parts, matrix, split, end_matrix)))
    return new_starts[None], fine_jumps[None]


def solution(mesh):
    in_specs = (P("tm", None, "space", None, None), P("tm", None, "space", None, None), P())
    out_specs = (P("tm", None, "space", None, None), P("tm", None, "space", None, None))
    return jax.shard_map(
        on_device, mesh=mesh, in_specs=in_specs, out_specs=out_specs, check_vma=False
    )
```

```python
import functools

import jax
import jax.numpy as jnp
from jax import lax
from jax.experimental import pallas as pl
from jax.experimental.pallas import tpu as pltpu
from jax.sharding import PartitionSpec as P

STEPS = 4
SOUND = 0.15
DIFFUSION = 0.08
HIGHEST = lax.Precision.HIGHEST
F32 = jnp.float32
PAUSE = 8000


def shaped(shape):
    return jax.ShapeDtypeStruct(shape, F32)


def cost(flops, nbytes):
    return pl.CostEstimate(flops=flops, bytes_accessed=nbytes, transcendentals=0)


def params(limit=16 << 20):
    return pltpu.CompilerParams(vmem_limit_bytes=limit)


def low_half():
    return lax.broadcasted_iota(jnp.int32, (16, 8, 128), 1) < 4


def to_chunks(first, second):
    one, two = first.reshape(16, 8, 128), second.reshape(16, 8, 128)
    low = low_half()
    even = jnp.where(low, one, pltpu.roll(two, 4, 1))
    odd = jnp.where(low, pltpu.roll(one, 4, 1), two)
    return even, odd


def from_chunks(even, odd):
    low = low_half()
    one = jnp.where(low, even, pltpu.roll(odd, 4, 1))
    two = jnp.where(low, pltpu.roll(even, 4, 1), odd)
    return one.reshape(128, 128), two.reshape(128, 128)


def chunk_kernel(pause, tile_ref, out_ref, tile, held, in_sems, out_sems):
    arriving = [pltpu.make_async_copy(tile_ref.at[field], tile.at[field], in_sems.at[field]) for field in range(3)]
    for copy in arriving:
        copy.start()
    if pause:

        @pl.when(lax.rem(lax.axis_index("space"), 2) == 1)
        def _():
            pl.delay(pause)

    leaving = []
    for pair in range(6):
        if pair % 2 == 0:
            arriving[pair // 2].wait()
        blocks = []
        for half in range(2):
            field, part = divmod(2 * pair + half, 4)
            blocks.append(tile[field, 4 * part : 4 * part + 4].reshape(128, 128).T)
        rows = slice(8 * pair, 8 * pair + 8)
        even, odd = to_chunks(blocks[0], blocks[1])
        held[:, 0, rows, :] = even
        held[:, 1, rows, :] = odd
        copy = pltpu.make_async_copy(held.at[:, :, rows], out_ref.at[:, :, rows], out_sems.at[pair])
        copy.start()
        leaving.append(copy)
    for copy in leaving:
        copy.wait()


def chunked(tile, pause=0):
    return pl.pallas_call(
        functools.partial(chunk_kernel, pause),
        out_shape=shaped((16, 2, 48, 128)),
        in_specs=[pl.BlockSpec(memory_space=pltpu.HBM)],
        out_specs=pl.BlockSpec(memory_space=pltpu.HBM),
        scratch_shapes=[
            pltpu.VMEM((3, 16, 32, 128), F32),
            pltpu.VMEM((16, 2, 48, 128), F32),
            pltpu.SemaphoreType.DMA((3,)),
            pltpu.SemaphoreType.DMA((6,)),
        ],
        name="chunked",
        cost_estimate=cost(0, 1600000),
        compiler_params=params(67000000) if pause else params(),
    )(tile)


def unchunk_kernel(chunks_ref, out_ref, held, sems):
    leaving = []
    for pair in range(6):
        rows = slice(8 * pair, 8 * pair + 8)
        blocks = from_chunks(chunks_ref[:, 0, rows, :], chunks_ref[:, 1, rows, :])
        field, part = divmod(2 * pair, 4)
        for half in range(2):
            layer = 4 * (part + half)
            held[field, layer : layer + 4] = blocks[half].T.reshape(4, 32, 128)
        layers = slice(4 * part, 4 * part + 8)
        copy = pltpu.make_async_copy(held.at[field, layers], out_ref.at[field, layers], sems.at[pair])
        copy.start()
        leaving.append(copy)
    for copy in leaving:
        copy.wait()


def unchunked(chunks):
    return pl.pallas_call(
        unchunk_kernel,
        out_shape=shaped((3, 16, 32, 128)),
        in_specs=[pl.BlockSpec(memory_space=pltpu.VMEM)],
        out_specs=pl.BlockSpec(memory_space=pltpu.HBM),
        scratch_shapes=[pltpu.VMEM((3, 16, 32, 128), F32), pltpu.SemaphoreType.DMA((6,))],
        name="unchunked",
        cost_estimate=cost(0, 1600000),
        compiler_params=params(),
    )(chunks)


def slab_kernel(chunks_ref, matrix_ref, slab_ref, first_ref, last_ref):
    for pair in range(6):
        rows = slice(8 * pair, 8 * pair + 8)
        blocks = from_chunks(chunks_ref[:, 0, rows, :], chunks_ref[:, 1, rows, :])
        for half in range(2):
            index = 2 * pair + half
            field, part = divmod(index, 4)
            matrix_ref[:, 128 * index : 128 * index + 128] = blocks[half]
            turned = blocks[half].T.reshape(4, 32, 128)
            slab_ref[field, 4 * part : 4 * part + 4] = turned
            if part == 0:
                first_ref[field] = turned
            if part == 3:
                last_ref[field] = turned


def slabbed(chunks):
    edge = (3, STEPS, 32, 128)
    return pl.pallas_call(
        slab_kernel,
        out_shape=(shaped((128, 1536)), shaped((3, 16, 32, 128)), shaped(edge), shaped(edge)),
        name="slabbed",
        cost_estimate=cost(0, 2800000), compiler_params=params(),
    )(chunks)


def advance(own_ref, before_ref, after_ref, speeds, ping, pong):
    ping[:, 0:4] = before_ref[...]
    ping[:, 4:20] = own_ref[...]
    ping[:, 20:24] = after_ref[...]
    drift_x, drift_y = 0.5 * speeds[0:1], 0.5 * speeds[1:2]
    held, fresh = ping, pong
    for step in range(STEPS):

        def layer(place, _, held=held, fresh=fresh):
            centre, east, west = held[:, place], held[:, place + 1], held[:, place - 1]
            north = pltpu.roll(centre, 31, 1)
            south = pltpu.roll(centre, 1, 1)
            diff_x, diff_y = east - west, north - south
            around = (east + west) + (north + south)
            moved = (1.0 - 4.0 * DIFFUSION) * centre + DIFFUSION * around - drift_x * diff_x - drift_y * diff_y
            half = 0.5 * SOUND
            fresh[0, place] = moved[0] - half * (diff_x[1] + diff_y[2])
            fresh[1, place] = moved[1] - half * diff_x[0]
            fresh[2, place] = moved[2] - half * diff_y[0]
            return 0

        lax.fori_loop(step + 1, 23 - step, layer, 0)
        held, fresh = fresh, held
    return held


def jump_kernel(own_ref, before_ref, after_ref, speeds_ref, ends_ref, out_ref, ping, pong):
    coarse = advance(own_ref, before_ref, after_ref, speeds_ref[...], ping, pong)
    out_ref[...] = ends_ref[...] - coarse[:, 4:20]


def fine_jumps_of(own, before, after, speeds, ends):
    return pl.pallas_call(
        jump_kernel,
        out_shape=shaped((3, 16, 32, 128)),
        scratch_shapes=[pltpu.VMEM((3, 24, 32, 128), F32)] * 2,
        name="fine_jumps",
        cost_estimate=cost(18000000, 2800000), compiler_params=params(),
    )(own, before, after, speeds, ends)


def iota(rows, lanes, axis):
    return lax.broadcasted_iota(jnp.int32, (rows, lanes), axis)


def where_one(test):
    return jnp.where(test, 1.0, 0.0).astype(F32)


def multiply(left, right):
    return jnp.dot(left, right, precision=HIGHEST, preferred_element_type=F32)


def pieces(value):
    first = value.astype(jnp.bfloat16)
    left = value - first.astype(F32)
    second = left.astype(jnp.bfloat16)
    third = (left - second.astype(F32)).astype(jnp.bfloat16)
    return first, second, third


def same_level():
    return (iota(128, 128, 0) & 3) == (iota(128, 128, 1) & 3)


def folded(product, place):
    pick = where_one((iota(32, 128, 1) >> 2) == iota(32, 128, 0))
    put = where_one((iota(128, 128, 0) >> 2) + 32 * place == iota(128, 128, 1))
    return multiply(multiply(pick, jnp.where(same_level(), product, 0.0)), put)


def packed(table):
    free = iota(8, 128, 1) >= 96
    return [
        jnp.where(free, pltpu.roll(table[24:32], 96 - 32 * part, 1), table[8 * part : 8 * part + 8])
        for part in range(3)
    ]


def unpacked(rows):
    group = iota(8, 128, 1) >> 5
    parts = [rows[8 * part : 8 * part + 8] for part in range(3)]
    moved = [pltpu.roll(parts[part], 32 + 32 * part, 1) for part in range(3)]
    last = jnp.where(group == 0, moved[0], jnp.where(group == 1, moved[1], moved[2]))
    return parts + [last]


def gram_kernel(matrix_ref, out_ref, pieces_ref):
    for index in range(12):
        lanes = slice(128 * index, 128 * index + 128)
        for place, piece in enumerate(pieces(matrix_ref[:, lanes])):
            pieces_ref[128 * place : 128 * place + 128, lanes] = piece
    matrix = matrix_ref[...]
    gram = lax.dot_general(matrix, matrix, (((1,), (1,)), ((), ())), precision=HIGHEST, preferred_element_type=F32)
    out_ref[...] = folded(gram, 0)


def gram_of(matrix):
    return pl.pallas_call(
        gram_kernel,
        out_shape=(shaped((32, 128)), jax.ShapeDtypeStruct((384, 1536), jnp.bfloat16)),
        name="gram",
        cost_estimate=cost(50000000, 2000000),
        compiler_params=params(),
    )(matrix)


def cross_kernel(own_ref, before_ref, after_ref, speeds_ref, matrix_ref, gram_ref, out_ref, ping, pong):
    first = 4 * lax.axis_index("tm")
    pick = where_one(iota(128, 128, 0) == first + (iota(128, 128, 1) & 3))
    coarse = advance(own_ref, before_ref, after_ref, multiply(speeds_ref[...], pick), ping, pong)
    cross = multiply(matrix_ref[...], coarse[:, 4:20].reshape(1536, 128))
    out_ref[...] = gram_ref[...] + folded(cross, 1)


def gram_and_cross(own, before, after, speeds, matrix, gram):
    return pl.pallas_call(
        cross_kernel,
        out_shape=shaped((32, 128)),
        scratch_shapes=[pltpu.VMEM((3, 24, 32, 128), F32)] * 2,
        name="gram_and_cross",
        cost_estimate=cost(18000000, 2800000),
        compiler_params=params(),
    )(own, before, after, speeds, matrix, gram)


def ends_kernel(chunks_ref, starts_ref, pair_ref, ends_ref, out_ref, split):
    for pair in range(6):
        rows = slice(8 * pair, 8 * pair + 8)
        blocks = from_chunks(chunks_ref[:, 0, rows, :], chunks_ref[:, 1, rows, :])
        for half in range(2):
            index = 2 * pair + half
            lanes = slice(128 * index, 128 * index + 128)
            ends_ref[:, lanes] = blocks[half]
            for place, piece in enumerate(pieces(blocks[half])):
                split[128 * place : 128 * place + 128, lanes] = piece

    def against(rows, columns):
        return lax.dot_general(
            starts_ref[0:rows], split[columns], (((1,), (1,)), ((), ())), preferred_element_type=F32
        )

    low, high = against(384, slice(0, 256)), against(128, slice(256, 384))
    product = (low[256:384, 0:128] + low[128:256, 128:256] + high) + (low[128:256, 0:128] + low[0:128, 128:256])
    product = product + low[0:128, 0:128]
    parts = packed(pair_ref[...] + folded(product, 2))
    for part in range(3):
        out_ref[:, 8 * part : 8 * part + 8, :] = jnp.broadcast_to(parts[part][None], (out_ref.shape[0], 8, 128))


def partial_sums(chunks, starts, pair, copies):
    return pl.pallas_call(
        ends_kernel,
        out_shape=(shaped((128, 1536)), shaped((copies, 24, 128))),
        scratch_shapes=[pltpu.VMEM((384, 1536), jnp.bfloat16)],
        name="partial_sums",
        cost_estimate=cost(50000000, 2800000), compiler_params=params(),
    )(chunks, starts, pair)


def total_kernel(parts_ref, out_ref):
    out_ref[...] = jnp.broadcast_to(jnp.sum(parts_ref[...], axis=0)[None], out_ref.shape)


def totals(parts, copies):
    return pl.pallas_call(
        total_kernel, out_shape=shaped((copies, 24, 128)), name="totals", cost_estimate=cost(100000, 600000), compiler_params=params()
    )(parts)


def eliminated(blocks):
    row = iota(8, 128, 0)
    for panel in range(4):
        columns = [
            [jnp.broadcast_to(block[:, 8 * panel + q : 8 * panel + q + 1], (8, 128)) for block in blocks]
            for q in range(8)
        ]
        for m in range(8):
            is_pivot = row == m
            column = columns[m]
            scale = 1.0 / column[panel][m : m + 1]

            def reduced(target):
                pivot = jnp.broadcast_to(target[panel][m : m + 1] * scale, (8, 128))
                return [
                    jnp.where(is_pivot, pivot, block - column[place] * pivot)
                    if place == panel
                    else block - column[place] * pivot
                    for place, block in enumerate(target)
                ]

            for q in range(m + 1, 8):
                columns[q] = reduced(columns[q])
            blocks = reduced(blocks)
    return blocks


def mixing_of(blocks):
    turned = jnp.concatenate(eliminated(blocks), axis=0).T
    power, moved = turned[32:64], turned[64:96]
    wide = multiply(power, where_one((iota(32, 128, 1) >> 2) == iota(32, 128, 0)))
    slice_of = iota(128, 32, 0) >> 2
    unit = where_one((slice_of == iota(128, 32, 1)) & (slice_of >= 1))
    change = multiply(where_one(slice_of == iota(128, 32, 1) + 1), moved) - unit

    def later(value, rows):
        return jnp.concatenate([jnp.zeros((rows, 32), F32), value[: 128 - rows]], axis=0)

    for level in range(5):
        change = change + multiply(later(change, 4 << level), power)
        if level < 4:
            power = multiply(power, power)
    return jnp.where(same_level(), multiply(later(change, 4), wide), 0.0)


def fresh_kernel(parts_ref, starts_ref, pieces_ref, ends_ref, out_ref, held, sems):
    one, two, three = pieces(mixing_of(unpacked(jnp.sum(parts_ref[...], axis=0))))
    mixing = jnp.concatenate([three, two, one, two, one, one], axis=1)
    first = iota(128, 256, 0) < 4
    copies = []
    for pair in range(6):
        columns = slice(256 * pair, 256 * pair + 256)
        starts = starts_ref[:, columns]
        prior = jnp.where(first, starts, pltpu.roll(ends_ref[:, columns], 4, 0))
        split = [pieces_ref[128 * place : 128 * place + 128, columns] for place in range(3)]
        split = jnp.concatenate([split[0], split[1], split[2], split[0], split[1], split[0]], axis=0)
        fresh = prior + jnp.dot(mixing, split, preferred_element_type=F32)
        even, odd = to_chunks(fresh[:, 0:128], fresh[:, 128:256])
        rows = slice(8 * pair, 8 * pair + 8)
        held[:, 0, rows, :] = even
        held[:, 1, rows, :] = odd
        copy = pltpu.make_async_copy(held.at[:, :, rows], out_ref.at[:, :, rows], sems.at[pair])
        copy.start()
        copies.append(copy)
    for copy in copies:
        copy.wait()


def fresh_chunks(parts, starts, split, ends):
    return pl.pallas_call(
        fresh_kernel,
        out_shape=shaped((16, 2, 48, 128)),
        in_specs=[pl.BlockSpec(memory_space=pltpu.VMEM)] * 4,
        out_specs=pl.BlockSpec(memory_space=pl.ANY),
        scratch_shapes=[pltpu.VMEM((16, 2, 48, 128), F32), pltpu.SemaphoreType.DMA((6,))],
        name="fresh_chunks",
        cost_estimate=cost(50000000, 2800000), compiler_params=params(),
    )(parts, starts, split, ends)


def exchanged(chunks):
    moved = lax.all_to_all(chunks.reshape(32, 48, 128), "tm", split_axis=0, concat_axis=0, tiled=True)
    return moved.reshape(16, 2, 48, 128)


def sides(first, last):
    size = lax.axis_size("space")
    up = [(i, (i + 1) % size) for i in range(size)]
    down = [(j, i) for i, j in up]
    return lax.ppermute(last, "space", up), lax.ppermute(first, "space", down)


def on_device(slice_starts, fine_ends, level_speeds):
    space = lax.axis_size("space")
    starts, ends = slice_starts[0], fine_ends[0]
    start_chunks = exchanged(chunked(starts, PAUSE))
    end_chunks = exchanged(chunked(ends))
    before, after = sides(starts[:, :STEPS], starts[:, -STEPS:])
    fine_jumps = fine_jumps_of(starts, before, after, level_speeds, ends)
    matrix, slab, first, last = slabbed(start_chunks)
    slab_before, slab_after = sides(first, last)
    gram, split = gram_of(matrix)
    pair = gram_and_cross(slab, slab_before, slab_after, level_speeds, matrix, gram)
    end_matrix, parts = partial_sums(end_chunks, split, pair, space)
    parts = lax.all_to_all(parts, "space", split_axis=0, concat_axis=0, tiled=True)
    parts = totals(parts, 32)
    parts = lax.all_to_all(parts, "tm", split_axis=0, concat_axis=0, tiled=True)
    new_starts = unchunked(exchanged(fresh_chunks(parts, matrix, split, end_matrix)))
    return new_starts[None], fine_jumps[None]


def solution(mesh):
    in_specs = (P("tm", None, "space", None, None), P("tm", None, "space", None, None), P())
    out_specs = (P("tm", None, "space", None, None), P("tm", None, "space", None, None))
    return jax.shard_map(
        on_device, mesh=mesh, in_specs=in_specs, out_specs=out_specs, check_vma=False
    )
```

```python
import functools

import jax
import jax.numpy as jnp
from jax import lax
from jax.experimental import pallas as pl
from jax.experimental.pallas import tpu as pltpu
from jax.sharding import PartitionSpec as P

STEPS = 4
SOUND = 0.15
DIFFUSION = 0.08
HIGHEST = lax.Precision.HIGHEST
F32 = jnp.float32
PAUSE = 10000


def shaped(shape):
    return jax.ShapeDtypeStruct(shape, F32)


def cost(flops, nbytes):
    return pl.CostEstimate(flops=flops, bytes_accessed=nbytes, transcendentals=0)


def params(limit=16 << 20):
    return pltpu.CompilerParams(vmem_limit_bytes=limit)


def low_half():
    return lax.broadcasted_iota(jnp.int32, (16, 8, 128), 1) < 4


def to_chunks(first, second):
    one, two = first.reshape(16, 8, 128), second.reshape(16, 8, 128)
    low = low_half()
    even = jnp.where(low, one, pltpu.roll(two, 4, 1))
    odd = jnp.where(low, pltpu.roll(one, 4, 1), two)
    return even, odd


def from_chunks(even, odd):
    low = low_half()
    one = jnp.where(low, even, pltpu.roll(odd, 4, 1))
    two = jnp.where(low, pltpu.roll(even, 4, 1), odd)
    return one.reshape(128, 128), two.reshape(128, 128)


def chunk_kernel(pause, tile_ref, out_ref, tile, held, in_sems, out_sems):
    arriving = [pltpu.make_async_copy(tile_ref.at[field], tile.at[field], in_sems.at[field]) for field in range(3)]
    for copy in arriving:
        copy.start()
    if pause:

        @pl.when(lax.rem(lax.axis_index("space"), 2) == 1)
        def _():
            pl.delay(pause)

    leaving = []
    for pair in range(6):
        if pair % 2 == 0:
            arriving[pair // 2].wait()
        blocks = []
        for half in range(2):
            field, part = divmod(2 * pair + half, 4)
            blocks.append(tile[field, 4 * part : 4 * part + 4].reshape(128, 128).T)
        rows = slice(8 * pair, 8 * pair + 8)
        even, odd = to_chunks(blocks[0], blocks[1])
        held[:, 0, rows, :] = even
        held[:, 1, rows, :] = odd
        copy = pltpu.make_async_copy(held.at[:, :, rows], out_ref.at[:, :, rows], out_sems.at[pair])
        copy.start()
        leaving.append(copy)
    for copy in leaving:
        copy.wait()


def chunked(tile, pause=0):
    return pl.pallas_call(
        functools.partial(chunk_kernel, pause),
        out_shape=shaped((16, 2, 48, 128)),
        in_specs=[pl.BlockSpec(memory_space=pltpu.HBM)],
        out_specs=pl.BlockSpec(memory_space=pltpu.HBM),
        scratch_shapes=[
            pltpu.VMEM((3, 16, 32, 128), F32),
            pltpu.VMEM((16, 2, 48, 128), F32),
            pltpu.SemaphoreType.DMA((3,)),
            pltpu.SemaphoreType.DMA((6,)),
        ],
        name="chunked",
        cost_estimate=cost(0, 1600000),
        compiler_params=params(67000000) if pause else params(),
    )(tile)


def unchunk_kernel(chunks_ref, out_ref, held, sems):
    leaving = []
    for pair in range(6):
        rows = slice(8 * pair, 8 * pair + 8)
        blocks = from_chunks(chunks_ref[:, 0, rows, :], chunks_ref[:, 1, rows, :])
        field, part = divmod(2 * pair, 4)
        for half in range(2):
            layer = 4 * (part + half)
            held[field, layer : layer + 4] = blocks[half].T.reshape(4, 32, 128)
        layers = slice(4 * part, 4 * part + 8)
        copy = pltpu.make_async_copy(held.at[field, layers], out_ref.at[field, layers], sems.at[pair])
        copy.start()
        leaving.append(copy)
    for copy in leaving:
        copy.wait()


def unchunked(chunks):
    return pl.pallas_call(
        unchunk_kernel,
        out_shape=shaped((3, 16, 32, 128)),
        in_specs=[pl.BlockSpec(memory_space=pltpu.VMEM)],
        out_specs=pl.BlockSpec(memory_space=pltpu.HBM),
        scratch_shapes=[pltpu.VMEM((3, 16, 32, 128), F32), pltpu.SemaphoreType.DMA((6,))],
        name="unchunked",
        cost_estimate=cost(0, 1600000),
        compiler_params=params(),
    )(chunks)


def slab_kernel(chunks_ref, matrix_ref, slab_ref, first_ref, last_ref):
    for pair in range(6):
        rows = slice(8 * pair, 8 * pair + 8)
        blocks = from_chunks(chunks_ref[:, 0, rows, :], chunks_ref[:, 1, rows, :])
        for half in range(2):
            index = 2 * pair + half
            field, part = divmod(index, 4)
            matrix_ref[:, 128 * index : 128 * index + 128] = blocks[half]
            turned = blocks[half].T.reshape(4, 32, 128)
            slab_ref[field, 4 * part : 4 * part + 4] = turned
            if part == 0:
                first_ref[field] = turned
            if part == 3:
                last_ref[field] = turned


def slabbed(chunks):
    edge = (3, STEPS, 32, 128)
    return pl.pallas_call(
        slab_kernel,
        out_shape=(shaped((128, 1536)), shaped((3, 16, 32, 128)), shaped(edge), shaped(edge)),
        name="slabbed",
        cost_estimate=cost(0, 2800000), compiler_params=params(),
    )(chunks)


def advance(own_ref, before_ref, after_ref, speeds, ping, pong):
    ping[:, 0:4] = before_ref[...]
    ping[:, 4:20] = own_ref[...]
    ping[:, 20:24] = after_ref[...]
    drift_x, drift_y = 0.5 * speeds[0:1], 0.5 * speeds[1:2]
    held, fresh = ping, pong
    for step in range(STEPS):

        def layer(place, _, held=held, fresh=fresh):
            centre, east, west = held[:, place], held[:, place + 1], held[:, place - 1]
            north = pltpu.roll(centre, 31, 1)
            south = pltpu.roll(centre, 1, 1)
            diff_x, diff_y = east - west, north - south
            around = (east + west) + (north + south)
            moved = (1.0 - 4.0 * DIFFUSION) * centre + DIFFUSION * around - drift_x * diff_x - drift_y * diff_y
            half = 0.5 * SOUND
            fresh[0, place] = moved[0] - half * (diff_x[1] + diff_y[2])
            fresh[1, place] = moved[1] - half * diff_x[0]
            fresh[2, place] = moved[2] - half * diff_y[0]
            return 0

        lax.fori_loop(step + 1, 23 - step, layer, 0)
        held, fresh = fresh, held
    return held


def jump_kernel(own_ref, before_ref, after_ref, speeds_ref, ends_ref, out_ref, ping, pong):
    coarse = advance(own_ref, before_ref, after_ref, speeds_ref[...], ping, pong)
    out_ref[...] = ends_ref[...] - coarse[:, 4:20]


def fine_jumps_of(own, before, after, speeds, ends):
    return pl.pallas_call(
        jump_kernel,
        out_shape=shaped((3, 16, 32, 128)),
        scratch_shapes=[pltpu.VMEM((3, 24, 32, 128), F32)] * 2,
        name="fine_jumps",
        cost_estimate=cost(18000000, 2800000), compiler_params=params(),
    )(own, before, after, speeds, ends)


def iota(rows, lanes, axis):
    return lax.broadcasted_iota(jnp.int32, (rows, lanes), axis)


def where_one(test):
    return jnp.where(test, 1.0, 0.0).astype(F32)


def multiply(left, right):
    return jnp.dot(left, right, precision=HIGHEST, preferred_element_type=F32)


def pieces(value):
    first = value.astype(jnp.bfloat16)
    left = value - first.astype(F32)
    second = left.astype(jnp.bfloat16)
    third = (left - second.astype(F32)).astype(jnp.bfloat16)
    return first, second, third


def same_level():
    return (iota(128, 128, 0) & 3) == (iota(128, 128, 1) & 3)


def folded(product, place):
    pick = where_one((iota(32, 128, 1) >> 2) == iota(32, 128, 0))
    put = where_one((iota(128, 128, 0) >> 2) + 32 * place == iota(128, 128, 1))
    return multiply(multiply(pick, jnp.where(same_level(), product, 0.0)), put)


def packed(table):
    free = iota(8, 128, 1) >= 96
    return [
        jnp.where(free, pltpu.roll(table[24:32], 96 - 32 * part, 1), table[8 * part : 8 * part + 8])
        for part in range(3)
    ]


def unpacked(rows):
    group = iota(8, 128, 1) >> 5
    parts = [rows[8 * part : 8 * part + 8] for part in range(3)]
    moved = [pltpu.roll(parts[part], 32 + 32 * part, 1) for part in range(3)]
    last = jnp.where(group == 0, moved[0], jnp.where(group == 1, moved[1], moved[2]))
    return parts + [last]


def gram_kernel(matrix_ref, out_ref, pieces_ref):
    for index in range(12):
        lanes = slice(128 * index, 128 * index + 128)
        for place, piece in enumerate(pieces(matrix_ref[:, lanes])):
            pieces_ref[128 * place : 128 * place + 128, lanes] = piece
    matrix = matrix_ref[...]
    gram = lax.dot_general(matrix, matrix, (((1,), (1,)), ((), ())), precision=HIGHEST, preferred_element_type=F32)
    out_ref[...] = folded(gram, 0)


def gram_of(matrix):
    return pl.pallas_call(
        gram_kernel,
        out_shape=(shaped((32, 128)), jax.ShapeDtypeStruct((384, 1536), jnp.bfloat16)),
        name="gram",
        cost_estimate=cost(50000000, 2000000),
        compiler_params=params(),
    )(matrix)


def cross_kernel(own_ref, before_ref, after_ref, speeds_ref, matrix_ref, gram_ref, out_ref, ping, pong):
    first = 4 * lax.axis_index("tm")
    pick = where_one(iota(128, 128, 0) == first + (iota(128, 128, 1) & 3))
    coarse = advance(own_ref, before_ref, after_ref, multiply(speeds_ref[...], pick), ping, pong)
    cross = multiply(matrix_ref[...], coarse[:, 4:20].reshape(1536, 128))
    out_ref[...] = gram_ref[...] + folded(cross, 1)


def gram_and_cross(own, before, after, speeds, matrix, gram):
    return pl.pallas_call(
        cross_kernel,
        out_shape=shaped((32, 128)),
        scratch_shapes=[pltpu.VMEM((3, 24, 32, 128), F32)] * 2,
        name="gram_and_cross",
        cost_estimate=cost(18000000, 2800000),
        compiler_params=params(),
    )(own, before, after, speeds, matrix, gram)


def ends_kernel(chunks_ref, starts_ref, pair_ref, ends_ref, out_ref, split):
    for pair in range(6):
        rows = slice(8 * pair, 8 * pair + 8)
        blocks = from_chunks(chunks_ref[:, 0, rows, :], chunks_ref[:, 1, rows, :])
        for half in range(2):
            index = 2 * pair + half
            lanes = slice(128 * index, 128 * index + 128)
            ends_ref[:, lanes] = blocks[half]
            for place, piece in enumerate(pieces(blocks[half])):
                split[128 * place : 128 * place + 128, lanes] = piece

    def against(rows, columns):
        return lax.dot_general(
            starts_ref[0:rows], split[columns], (((1,), (1,)), ((), ())), preferred_element_type=F32
        )

    low, high = against(384, slice(0, 256)), against(128, slice(256, 384))
    product = (low[256:384, 0:128] + low[128:256, 128:256] + high) + (low[128:256, 0:128] + low[0:128, 128:256])
    product = product + low[0:128, 0:128]
    parts = packed(pair_ref[...] + folded(product, 2))
    for part in range(3):
        out_ref[:, 8 * part : 8 * part + 8, :] = jnp.broadcast_to(parts[part][None], (out_ref.shape[0], 8, 128))


def partial_sums(chunks, starts, pair, copies):
    return pl.pallas_call(
        ends_kernel,
        out_shape=(shaped((128, 1536)), shaped((copies, 24, 128))),
        scratch_shapes=[pltpu.VMEM((384, 1536), jnp.bfloat16)],
        name="partial_sums",
        cost_estimate=cost(50000000, 2800000), compiler_params=params(),
    )(chunks, starts, pair)


def total_kernel(parts_ref, out_ref):
    out_ref[...] = jnp.broadcast_to(jnp.sum(parts_ref[...], axis=0)[None], out_ref.shape)


def totals(parts, copies):
    return pl.pallas_call(
        total_kernel, out_shape=shaped((copies, 24, 128)), name="totals", cost_estimate=cost(100000, 600000), compiler_params=params()
    )(parts)


def eliminated(blocks):
    row = iota(8, 128, 0)
    for panel in range(4):
        columns = [
            [jnp.broadcast_to(block[:, 8 * panel + q : 8 * panel + q + 1], (8, 128)) for block in blocks]
            for q in range(8)
        ]
        for m in range(8):
            is_pivot = row == m
            column = columns[m]
            scale = 1.0 / column[panel][m : m + 1]

            def reduced(target):
                pivot = jnp.broadcast_to(target[panel][m : m + 1] * scale, (8, 128))
                return [
                    jnp.where(is_pivot, pivot, block - column[place] * pivot)
                    if place == panel
                    else block - column[place] * pivot
                    for place, block in enumerate(target)
                ]

            for q in range(m + 1, 8):
                columns[q] = reduced(columns[q])
            blocks = reduced(blocks)
    return blocks


def mixing_of(blocks):
    turned = jnp.concatenate(eliminated(blocks), axis=0).T
    power, moved = turned[32:64], turned[64:96]
    wide = multiply(power, where_one((iota(32, 128, 1) >> 2) == iota(32, 128, 0)))
    slice_of = iota(128, 32, 0) >> 2
    unit = where_one((slice_of == iota(128, 32, 1)) & (slice_of >= 1))
    change = multiply(where_one(slice_of == iota(128, 32, 1) + 1), moved) - unit

    def later(value, rows):
        return jnp.concatenate([jnp.zeros((rows, 32), F32), value[: 128 - rows]], axis=0)

    for level in range(5):
        change = change + multiply(later(change, 4 << level), power)
        if level < 4:
            power = multiply(power, power)
    return jnp.where(same_level(), multiply(later(change, 4), wide), 0.0)


def fresh_kernel(parts_ref, starts_ref, pieces_ref, ends_ref, out_ref, held, sems):
    one, two, three = pieces(mixing_of(unpacked(jnp.sum(parts_ref[...], axis=0))))
    mixing = jnp.concatenate([three, two, one, two, one, one], axis=1)
    first = iota(128, 256, 0) < 4
    copies = []
    for pair in range(6):
        columns = slice(256 * pair, 256 * pair + 256)
        starts = starts_ref[:, columns]
        prior = jnp.where(first, starts, pltpu.roll(ends_ref[:, columns], 4, 0))
        split = [pieces_ref[128 * place : 128 * place + 128, columns] for place in range(3)]
        split = jnp.concatenate([split[0], split[1], split[2], split[0], split[1], split[0]], axis=0)
        fresh = prior + jnp.dot(mixing, split, preferred_element_type=F32)
        even, odd = to_chunks(fresh[:, 0:128], fresh[:, 128:256])
        rows = slice(8 * pair, 8 * pair + 8)
        held[:, 0, rows, :] = even
        held[:, 1, rows, :] = odd
        copy = pltpu.make_async_copy(held.at[:, :, rows], out_ref.at[:, :, rows], sems.at[pair])
        copy.start()
        copies.append(copy)
    for copy in copies:
        copy.wait()


def fresh_chunks(parts, starts, split, ends):
    return pl.pallas_call(
        fresh_kernel,
        out_shape=shaped((16, 2, 48, 128)),
        in_specs=[pl.BlockSpec(memory_space=pltpu.VMEM)] * 4,
        out_specs=pl.BlockSpec(memory_space=pl.ANY),
        scratch_shapes=[pltpu.VMEM((16, 2, 48, 128), F32), pltpu.SemaphoreType.DMA((6,))],
        name="fresh_chunks",
        cost_estimate=cost(50000000, 2800000), compiler_params=params(),
    )(parts, starts, split, ends)


def exchanged(chunks):
    moved = lax.all_to_all(chunks.reshape(32, 48, 128), "tm", split_axis=0, concat_axis=0, tiled=True)
    return moved.reshape(16, 2, 48, 128)


def sides(first, last):
    size = lax.axis_size("space")
    up = [(i, (i + 1) % size) for i in range(size)]
    down = [(j, i) for i, j in up]
    return lax.ppermute(last, "space", up), lax.ppermute(first, "space", down)


def on_device(slice_starts, fine_ends, level_speeds):
    space = lax.axis_size("space")
    starts, ends = slice_starts[0], fine_ends[0]
    start_chunks = exchanged(chunked(starts, PAUSE))
    end_chunks = exchanged(chunked(ends))
    before, after = sides(starts[:, :STEPS], starts[:, -STEPS:])
    fine_jumps = fine_jumps_of(starts, before, after, level_speeds, ends)
    matrix, slab, first, last = slabbed(start_chunks)
    slab_before, slab_after = sides(first, last)
    gram, split = gram_of(matrix)
    pair = gram_and_cross(slab, slab_before, slab_after, level_speeds, matrix, gram)
    end_matrix, parts = partial_sums(end_chunks, split, pair, space)
    parts = lax.all_to_all(parts, "space", split_axis=0, concat_axis=0, tiled=True)
    parts = totals(parts, 32)
    parts = lax.all_to_all(parts, "tm", split_axis=0, concat_axis=0, tiled=True)
    new_starts = unchunked(exchanged(fresh_chunks(parts, matrix, split, end_matrix)))
    return new_starts[None], fine_jumps[None]


def solution(mesh):
    in_specs = (P("tm", None, "space", None, None), P("tm", None, "space", None, None), P())
    out_specs = (P("tm", None, "space", None, None), P("tm", None, "space", None, None))
    return jax.shard_map(
        on_device, mesh=mesh, in_specs=in_specs, out_specs=out_specs, check_vma=False
    )
```

```python
import functools

import jax
import jax.numpy as jnp
from jax import lax
from jax.experimental import pallas as pl
from jax.experimental.pallas import tpu as pltpu
from jax.sharding import PartitionSpec as P

STEPS = 4
SOUND = 0.15
DIFFUSION = 0.08
HIGHEST = lax.Precision.HIGHEST
F32 = jnp.float32
PAUSE = 12500


def shaped(shape):
    return jax.ShapeDtypeStruct(shape, F32)


def cost(flops, nbytes):
    return pl.CostEstimate(flops=flops, bytes_accessed=nbytes, transcendentals=0)


def params(limit=16 << 20):
    return pltpu.CompilerParams(vmem_limit_bytes=limit)


def low_half():
    return lax.broadcasted_iota(jnp.int32, (16, 8, 128), 1) < 4


def to_chunks(first, second):
    one, two = first.reshape(16, 8, 128), second.reshape(16, 8, 128)
    low = low_half()
    even = jnp.where(low, one, pltpu.roll(two, 4, 1))
    odd = jnp.where(low, pltpu.roll(one, 4, 1), two)
    return even, odd


def from_chunks(even, odd):
    low = low_half()
    one = jnp.where(low, even, pltpu.roll(odd, 4, 1))
    two = jnp.where(low, pltpu.roll(even, 4, 1), odd)
    return one.reshape(128, 128), two.reshape(128, 128)


def chunk_kernel(pause, tile_ref, out_ref, tile, held, in_sems, out_sems):
    arriving = [pltpu.make_async_copy(tile_ref.at[field], tile.at[field], in_sems.at[field]) for field in range(3)]
    for copy in arriving:
        copy.start()
    if pause:

        @pl.when(lax.rem(lax.axis_index("space"), 2) == 1)
        def _():
            pl.delay(pause)

    leaving = []
    for pair in range(6):
        if pair % 2 == 0:
            arriving[pair // 2].wait()
        blocks = []
        for half in range(2):
            field, part = divmod(2 * pair + half, 4)
            blocks.append(tile[field, 4 * part : 4 * part + 4].reshape(128, 128).T)
        rows = slice(8 * pair, 8 * pair + 8)
        even, odd = to_chunks(blocks[0], blocks[1])
        held[:, 0, rows, :] = even
        held[:, 1, rows, :] = odd
        copy = pltpu.make_async_copy(held.at[:, :, rows], out_ref.at[:, :, rows], out_sems.at[pair])
        copy.start()
        leaving.append(copy)
    for copy in leaving:
        copy.wait()


def chunked(tile, pause=0):
    return pl.pallas_call(
        functools.partial(chunk_kernel, pause),
        out_shape=shaped((16, 2, 48, 128)),
        in_specs=[pl.BlockSpec(memory_space=pltpu.HBM)],
        out_specs=pl.BlockSpec(memory_space=pltpu.HBM),
        scratch_shapes=[
            pltpu.VMEM((3, 16, 32, 128), F32),
            pltpu.VMEM((16, 2, 48, 128), F32),
            pltpu.SemaphoreType.DMA((3,)),
            pltpu.SemaphoreType.DMA((6,)),
        ],
        name="chunked",
        cost_estimate=cost(0, 1600000),
        compiler_params=params(67000000) if pause else params(),
    )(tile)


def unchunk_kernel(chunks_ref, out_ref, held, sems):
    leaving = []
    for pair in range(6):
        rows = slice(8 * pair, 8 * pair + 8)
        blocks = from_chunks(chunks_ref[:, 0, rows, :], chunks_ref[:, 1, rows, :])
        field, part = divmod(2 * pair, 4)
        for half in range(2):
            layer = 4 * (part + half)
            held[field, layer : layer + 4] = blocks[half].T.reshape(4, 32, 128)
        layers = slice(4 * part, 4 * part + 8)
        copy = pltpu.make_async_copy(held.at[field, layers], out_ref.at[field, layers], sems.at[pair])
        copy.start()
        leaving.append(copy)
    for copy in leaving:
        copy.wait()


def unchunked(chunks):
    return pl.pallas_call(
        unchunk_kernel,
        out_shape=shaped((3, 16, 32, 128)),
        in_specs=[pl.BlockSpec(memory_space=pltpu.VMEM)],
        out_specs=pl.BlockSpec(memory_space=pltpu.HBM),
        scratch_shapes=[pltpu.VMEM((3, 16, 32, 128), F32), pltpu.SemaphoreType.DMA((6,))],
        name="unchunked",
        cost_estimate=cost(0, 1600000),
        compiler_params=params(),
    )(chunks)


def slab_kernel(chunks_ref, matrix_ref, slab_ref, first_ref, last_ref):
    for pair in range(6):
        rows = slice(8 * pair, 8 * pair + 8)
        blocks = from_chunks(chunks_ref[:, 0, rows, :], chunks_ref[:, 1, rows, :])
        for half in range(2):
            index = 2 * pair + half
            field, part = divmod(index, 4)
            matrix_ref[:, 128 * index : 128 * index + 128] = blocks[half]
            turned = blocks[half].T.reshape(4, 32, 128)
            slab_ref[field, 4 * part : 4 * part + 4] = turned
            if part == 0:
                first_ref[field] = turned
            if part == 3:
                last_ref[field] = turned


def slabbed(chunks):
    edge = (3, STEPS, 32, 128)
    return pl.pallas_call(
        slab_kernel,
        out_shape=(shaped((128, 1536)), shaped((3, 16, 32, 128)), shaped(edge), shaped(edge)),
        name="slabbed",
        cost_estimate=cost(0, 2800000), compiler_params=params(),
    )(chunks)


def advance(own_ref, before_ref, after_ref, speeds, ping, pong):
    ping[:, 0:4] = before_ref[...]
    ping[:, 4:20] = own_ref[...]
    ping[:, 20:24] = after_ref[...]
    drift_x, drift_y = 0.5 * speeds[0:1], 0.5 * speeds[1:2]
    held, fresh = ping, pong
    for step in range(STEPS):

        def layer(place, _, held=held, fresh=fresh):
            centre, east, west = held[:, place], held[:, place + 1], held[:, place - 1]
            north = pltpu.roll(centre, 31, 1)
            south = pltpu.roll(centre, 1, 1)
            diff_x, diff_y = east - west, north - south
            around = (east + west) + (north + south)
            moved = (1.0 - 4.0 * DIFFUSION) * centre + DIFFUSION * around - drift_x * diff_x - drift_y * diff_y
            half = 0.5 * SOUND
            fresh[0, place] = moved[0] - half * (diff_x[1] + diff_y[2])
            fresh[1, place] = moved[1] - half * diff_x[0]
            fresh[2, place] = moved[2] - half * diff_y[0]
            return 0

        lax.fori_loop(step + 1, 23 - step, layer, 0)
        held, fresh = fresh, held
    return held


def jump_kernel(own_ref, before_ref, after_ref, speeds_ref, ends_ref, out_ref, ping, pong):
    coarse = advance(own_ref, before_ref, after_ref, speeds_ref[...], ping, pong)
    out_ref[...] = ends_ref[...] - coarse[:, 4:20]


def fine_jumps_of(own, before, after, speeds, ends):
    return pl.pallas_call(
        jump_kernel,
        out_shape=shaped((3, 16, 32, 128)),
        scratch_shapes=[pltpu.VMEM((3, 24, 32, 128), F32)] * 2,
        name="fine_jumps",
        cost_estimate=cost(18000000, 2800000), compiler_params=params(),
    )(own, before, after, speeds, ends)


def iota(rows, lanes, axis):
    return lax.broadcasted_iota(jnp.int32, (rows, lanes), axis)


def where_one(test):
    return jnp.where(test, 1.0, 0.0).astype(F32)


def multiply(left, right):
    return jnp.dot(left, right, precision=HIGHEST, preferred_element_type=F32)


def pieces(value):
    first = value.astype(jnp.bfloat16)
    left = value - first.astype(F32)
    second = left.astype(jnp.bfloat16)
    third = (left - second.astype(F32)).astype(jnp.bfloat16)
    return first, second, third


def same_level():
    return (iota(128, 128, 0) & 3) == (iota(128, 128, 1) & 3)


def folded(product, place):
    pick = where_one((iota(32, 128, 1) >> 2) == iota(32, 128, 0))
    put = where_one((iota(128, 128, 0) >> 2) + 32 * place == iota(128, 128, 1))
    return multiply(multiply(pick, jnp.where(same_level(), product, 0.0)), put)


def packed(table):
    free = iota(8, 128, 1) >= 96
    return [
        jnp.where(free, pltpu.roll(table[24:32], 96 - 32 * part, 1), table[8 * part : 8 * part + 8])
        for part in range(3)
    ]


def unpacked(rows):
    group = iota(8, 128, 1) >> 5
    parts = [rows[8 * part : 8 * part + 8] for part in range(3)]
    moved = [pltpu.roll(parts[part], 32 + 32 * part, 1) for part in range(3)]
    last = jnp.where(group == 0, moved[0], jnp.where(group == 1, moved[1], moved[2]))
    return parts + [last]


def gram_kernel(matrix_ref, out_ref, pieces_ref):
    for index in range(12):
        lanes = slice(128 * index, 128 * index + 128)
        for place, piece in enumerate(pieces(matrix_ref[:, lanes])):
            pieces_ref[128 * place : 128 * place + 128, lanes] = piece
    matrix = matrix_ref[...]
    gram = lax.dot_general(matrix, matrix, (((1,), (1,)), ((), ())), precision=HIGHEST, preferred_element_type=F32)
    out_ref[...] = folded(gram, 0)


def gram_of(matrix):
    return pl.pallas_call(
        gram_kernel,
        out_shape=(shaped((32, 128)), jax.ShapeDtypeStruct((384, 1536), jnp.bfloat16)),
        name="gram",
        cost_estimate=cost(50000000, 2000000),
        compiler_params=params(),
    )(matrix)


def cross_kernel(own_ref, before_ref, after_ref, speeds_ref, matrix_ref, gram_ref, out_ref, ping, pong):
    first = 4 * lax.axis_index("tm")
    pick = where_one(iota(128, 128, 0) == first + (iota(128, 128, 1) & 3))
    coarse = advance(own_ref, before_ref, after_ref, multiply(speeds_ref[...], pick), ping, pong)
    cross = multiply(matrix_ref[...], coarse[:, 4:20].reshape(1536, 128))
    out_ref[...] = gram_ref[...] + folded(cross, 1)


def gram_and_cross(own, before, after, speeds, matrix, gram):
    return pl.pallas_call(
        cross_kernel,
        out_shape=shaped((32, 128)),
        scratch_shapes=[pltpu.VMEM((3, 24, 32, 128), F32)] * 2,
        name="gram_and_cross",
        cost_estimate=cost(18000000, 2800000),
        compiler_params=params(),
    )(own, before, after, speeds, matrix, gram)


def ends_kernel(chunks_ref, starts_ref, pair_ref, ends_ref, out_ref, split):
    for pair in range(6):
        rows = slice(8 * pair, 8 * pair + 8)
        blocks = from_chunks(chunks_ref[:, 0, rows, :], chunks_ref[:, 1, rows, :])
        for half in range(2):
            index = 2 * pair + half
            lanes = slice(128 * index, 128 * index + 128)
            ends_ref[:, lanes] = blocks[half]
            for place, piece in enumerate(pieces(blocks[half])):
                split[128 * place : 128 * place + 128, lanes] = piece

    def against(rows, columns):
        return lax.dot_general(
            starts_ref[0:rows], split[columns], (((1,), (1,)), ((), ())), preferred_element_type=F32
        )

    low, high = against(384, slice(0, 256)), against(128, slice(256, 384))
    product = (low[256:384, 0:128] + low[128:256, 128:256] + high) + (low[128:256, 0:128] + low[0:128, 128:256])
    product = product + low[0:128, 0:128]
    parts = packed(pair_ref[...] + folded(product, 2))
    for part in range(3):
        out_ref[:, 8 * part : 8 * part + 8, :] = jnp.broadcast_to(parts[part][None], (out_ref.shape[0], 8, 128))


def partial_sums(chunks, starts, pair, copies):
    return pl.pallas_call(
        ends_kernel,
        out_shape=(shaped((128, 1536)), shaped((copies, 24, 128))),
        scratch_shapes=[pltpu.VMEM((384, 1536), jnp.bfloat16)],
        name="partial_sums",
        cost_estimate=cost(50000000, 2800000), compiler_params=params(),
    )(chunks, starts, pair)


def total_kernel(parts_ref, out_ref):
    out_ref[...] = jnp.broadcast_to(jnp.sum(parts_ref[...], axis=0)[None], out_ref.shape)


def totals(parts, copies):
    return pl.pallas_call(
        total_kernel, out_shape=shaped((copies, 24, 128)), name="totals", cost_estimate=cost(100000, 600000), compiler_params=params()
    )(parts)


def eliminated(blocks):
    row = iota(8, 128, 0)
    for panel in range(4):
        columns = [
            [jnp.broadcast_to(block[:, 8 * panel + q : 8 * panel + q + 1], (8, 128)) for block in blocks]
            for q in range(8)
        ]
        for m in range(8):
            is_pivot = row == m
            column = columns[m]
            scale = 1.0 / column[panel][m : m + 1]

            def reduced(target):
                pivot = jnp.broadcast_to(target[panel][m : m + 1] * scale, (8, 128))
                return [
                    jnp.where(is_pivot, pivot, block - column[place] * pivot)
                    if place == panel
                    else block - column[place] * pivot
                    for place, block in enumerate(target)
                ]

            for q in range(m + 1, 8):
                columns[q] = reduced(columns[q])
            blocks = reduced(blocks)
    return blocks


def mixing_of(blocks):
    turned = jnp.concatenate(eliminated(blocks), axis=0).T
    power, moved = turned[32:64], turned[64:96]
    wide = multiply(power, where_one((iota(32, 128, 1) >> 2) == iota(32, 128, 0)))
    slice_of = iota(128, 32, 0) >> 2
    unit = where_one((slice_of == iota(128, 32, 1)) & (slice_of >= 1))
    change = multiply(where_one(slice_of == iota(128, 32, 1) + 1), moved) - unit

    def later(value, rows):
        return jnp.concatenate([jnp.zeros((rows, 32), F32), value[: 128 - rows]], axis=0)

    for level in range(5):
        change = change + multiply(later(change, 4 << level), power)
        if level < 4:
            power = multiply(power, power)
    return jnp.where(same_level(), multiply(later(change, 4), wide), 0.0)


def fresh_kernel(parts_ref, starts_ref, pieces_ref, ends_ref, out_ref, held, sems):
    one, two, three = pieces(mixing_of(unpacked(jnp.sum(parts_ref[...], axis=0))))
    mixing = jnp.concatenate([three, two, one, two, one, one], axis=1)
    first = iota(128, 256, 0) < 4
    copies = []
    for pair in range(6):
        columns = slice(256 * pair, 256 * pair + 256)
        starts = starts_ref[:, columns]
        prior = jnp.where(first, starts, pltpu.roll(ends_ref[:, columns], 4, 0))
        split = [pieces_ref[128 * place : 128 * place + 128, columns] for place in range(3)]
        split = jnp.concatenate([split[0], split[1], split[2], split[0], split[1], split[0]], axis=0)
        fresh = prior + jnp.dot(mixing, split, preferred_element_type=F32)
        even, odd = to_chunks(fresh[:, 0:128], fresh[:, 128:256])
        rows = slice(8 * pair, 8 * pair + 8)
        held[:, 0, rows, :] = even
        held[:, 1, rows, :] = odd
        copy = pltpu.make_async_copy(held.at[:, :, rows], out_ref.at[:, :, rows], sems.at[pair])
        copy.start()
        copies.append(copy)
    for copy in copies:
        copy.wait()


def fresh_chunks(parts, starts, split, ends):
    return pl.pallas_call(
        fresh_kernel,
        out_shape=shaped((16, 2, 48, 128)),
        in_specs=[pl.BlockSpec(memory_space=pltpu.VMEM)] * 4,
        out_specs=pl.BlockSpec(memory_space=pl.ANY),
        scratch_shapes=[pltpu.VMEM((16, 2, 48, 128), F32), pltpu.SemaphoreType.DMA((6,))],
        name="fresh_chunks",
        cost_estimate=cost(50000000, 2800000), compiler_params=params(),
    )(parts, starts, split, ends)


def exchanged(chunks):
    moved = lax.all_to_all(chunks.reshape(32, 48, 128), "tm", split_axis=0, concat_axis=0, tiled=True)
    return moved.reshape(16, 2, 48, 128)


def sides(first, last):
    size = lax.axis_size("space")
    up = [(i, (i + 1) % size) for i in range(size)]
    down = [(j, i) for i, j in up]
    return lax.ppermute(last, "space", up), lax.ppermute(first, "space", down)


def on_device(slice_starts, fine_ends, level_speeds):
    space = lax.axis_size("space")
    starts, ends = slice_starts[0], fine_ends[0]
    start_chunks = exchanged(chunked(starts, PAUSE))
    end_chunks = exchanged(chunked(ends))
    before, after = sides(starts[:, :STEPS], starts[:, -STEPS:])
    fine_jumps = fine_jumps_of(starts, before, after, level_speeds, ends)
    matrix, slab, first, last = slabbed(start_chunks)
    slab_before, slab_after = sides(first, last)
    gram, split = gram_of(matrix)
    pair = gram_and_cross(slab, slab_before, slab_after, level_speeds, matrix, gram)
    end_matrix, parts = partial_sums(end_chunks, split, pair, space)
    parts = lax.all_to_all(parts, "space", split_axis=0, concat_axis=0, tiled=True)
    parts = totals(parts, 32)
    parts = lax.all_to_all(parts, "tm", split_axis=0, concat_axis=0, tiled=True)
    new_starts = unchunked(exchanged(fresh_chunks(parts, matrix, split, end_matrix)))
    return new_starts[None], fine_jumps[None]


def solution(mesh):
    in_specs = (P("tm", None, "space", None, None), P("tm", None, "space", None, None), P())
    out_specs = (P("tm", None, "space", None, None), P("tm", None, "space", None, None))
    return jax.shard_map(
        on_device, mesh=mesh, in_specs=in_specs, out_specs=out_specs, check_vma=False
    )
```

```python
import functools

import jax
import jax.numpy as jnp
from jax import lax
from jax.experimental import pallas as pl
from jax.experimental.pallas import tpu as pltpu
from jax.sharding import PartitionSpec as P

STEPS = 4
SOUND = 0.15
DIFFUSION = 0.08
HIGHEST = lax.Precision.HIGHEST
F32 = jnp.float32
PAUSE = 12500


def shaped(shape):
    return jax.ShapeDtypeStruct(shape, F32)


def cost(flops, nbytes):
    return pl.CostEstimate(flops=flops, bytes_accessed=nbytes, transcendentals=0)


def params(limit=16 << 20):
    return pltpu.CompilerParams(vmem_limit_bytes=limit)


def low_half():
    return lax.broadcasted_iota(jnp.int32, (16, 8, 128), 1) < 4


def to_chunks(first, second):
    one, two = first.reshape(16, 8, 128), second.reshape(16, 8, 128)
    low = low_half()
    even = jnp.where(low, one, pltpu.roll(two, 4, 1))
    odd = jnp.where(low, pltpu.roll(one, 4, 1), two)
    return even, odd


def from_chunks(even, odd):
    low = low_half()
    one = jnp.where(low, even, pltpu.roll(odd, 4, 1))
    two = jnp.where(low, pltpu.roll(even, 4, 1), odd)
    return one.reshape(128, 128), two.reshape(128, 128)


def chunk_kernel(pause, tile_ref, out_ref, tile, held, in_sems, out_sems):
    arriving = [pltpu.make_async_copy(tile_ref.at[field], tile.at[field], in_sems.at[field]) for field in range(3)]
    for copy in arriving:
        copy.start()
    if pause:

        @pl.when(lax.rem(lax.axis_index("space"), 2) == 1)
        def _():
            pl.delay(pause)

    leaving = []
    for pair in range(6):
        if pair % 2 == 0:
            arriving[pair // 2].wait()
        blocks = []
        for half in range(2):
            field, part = divmod(2 * pair + half, 4)
            blocks.append(tile[field, 4 * part : 4 * part + 4].reshape(128, 128).T)
        rows = slice(8 * pair, 8 * pair + 8)
        even, odd = to_chunks(blocks[0], blocks[1])
        held[:, 0, rows, :] = even
        held[:, 1, rows, :] = odd
        copy = pltpu.make_async_copy(held.at[:, :, rows], out_ref.at[:, :, rows], out_sems.at[pair])
        copy.start()
        leaving.append(copy)
    for copy in leaving:
        copy.wait()


def chunked(tile, pause=0):
    return pl.pallas_call(
        functools.partial(chunk_kernel, pause),
        out_shape=shaped((16, 2, 48, 128)),
        in_specs=[pl.BlockSpec(memory_space=pltpu.HBM)],
        out_specs=pl.BlockSpec(memory_space=pltpu.HBM),
        scratch_shapes=[
            pltpu.VMEM((3, 16, 32, 128), F32),
            pltpu.VMEM((16, 2, 48, 128), F32),
            pltpu.SemaphoreType.DMA((3,)),
            pltpu.SemaphoreType.DMA((6,)),
        ],
        name="chunked",
        cost_estimate=cost(0, 1600000),
        compiler_params=params(67000000) if pause else params(),
    )(tile)


def unchunk_kernel(chunks_ref, out_ref, held, sems):
    leaving = []
    for pair in range(6):
        rows = slice(8 * pair, 8 * pair + 8)
        blocks = from_chunks(chunks_ref[:, 0, rows, :], chunks_ref[:, 1, rows, :])
        field, part = divmod(2 * pair, 4)
        for half in range(2):
            layer = 4 * (part + half)
            held[field, layer : layer + 4] = blocks[half].T.reshape(4, 32, 128)
        layers = slice(4 * part, 4 * part + 8)
        copy = pltpu.make_async_copy(held.at[field, layers], out_ref.at[field, layers], sems.at[pair])
        copy.start()
        leaving.append(copy)
    for copy in leaving:
        copy.wait()


def unchunked(chunks):
    return pl.pallas_call(
        unchunk_kernel,
        out_shape=shaped((3, 16, 32, 128)),
        in_specs=[pl.BlockSpec(memory_space=pltpu.VMEM)],
        out_specs=pl.BlockSpec(memory_space=pltpu.HBM),
        scratch_shapes=[pltpu.VMEM((3, 16, 32, 128), F32), pltpu.SemaphoreType.DMA((6,))],
        name="unchunked",
        cost_estimate=cost(0, 1600000),
        compiler_params=params(),
    )(chunks)


def slab_kernel(chunks_ref, matrix_ref, slab_ref, first_ref, last_ref):
    for pair in range(6):
        rows = slice(8 * pair, 8 * pair + 8)
        blocks = from_chunks(chunks_ref[:, 0, rows, :], chunks_ref[:, 1, rows, :])
        for half in range(2):
            index = 2 * pair + half
            field, part = divmod(index, 4)
            matrix_ref[:, 128 * index : 128 * index + 128] = blocks[half]
            turned = blocks[half].T.reshape(4, 32, 128)
            slab_ref[field, 4 * part : 4 * part + 4] = turned
            if part == 0:
                first_ref[field] = turned
            if part == 3:
                last_ref[field] = turned


def slabbed(chunks):
    edge = (3, STEPS, 32, 128)
    return pl.pallas_call(
        slab_kernel,
        out_shape=(shaped((128, 1536)), shaped((3, 16, 32, 128)), shaped(edge), shaped(edge)),
        name="slabbed",
        cost_estimate=cost(0, 2800000), compiler_params=params(),
    )(chunks)


def advance(own_ref, before_ref, after_ref, speeds, ping, pong):
    ping[:, 0:4] = before_ref[...]
    ping[:, 4:20] = own_ref[...]
    ping[:, 20:24] = after_ref[...]
    drift_x, drift_y = 0.5 * speeds[0:1], 0.5 * speeds[1:2]
    held, fresh = ping, pong
    for step in range(STEPS):

        def layer(place, _, held=held, fresh=fresh):
            centre, east, west = held[:, place], held[:, place + 1], held[:, place - 1]
            north = pltpu.roll(centre, 31, 1)
            south = pltpu.roll(centre, 1, 1)
            diff_x, diff_y = east - west, north - south
            around = (east + west) + (north + south)
            moved = (1.0 - 4.0 * DIFFUSION) * centre + DIFFUSION * around - drift_x * diff_x - drift_y * diff_y
            half = 0.5 * SOUND
            fresh[0, place] = moved[0] - half * (diff_x[1] + diff_y[2])
            fresh[1, place] = moved[1] - half * diff_x[0]
            fresh[2, place] = moved[2] - half * diff_y[0]
            return 0

        lax.fori_loop(step + 1, 23 - step, layer, 0)
        held, fresh = fresh, held
    return held


def jump_kernel(own_ref, before_ref, after_ref, speeds_ref, ends_ref, out_ref, ping, pong):
    coarse = advance(own_ref, before_ref, after_ref, speeds_ref[...], ping, pong)
    out_ref[...] = ends_ref[...] - coarse[:, 4:20]


def fine_jumps_of(own, before, after, speeds, ends):
    return pl.pallas_call(
        jump_kernel,
        out_shape=shaped((3, 16, 32, 128)),
        scratch_shapes=[pltpu.VMEM((3, 24, 32, 128), F32)] * 2,
        name="fine_jumps",
        cost_estimate=cost(18000000, 2800000), compiler_params=params(),
    )(own, before, after, speeds, ends)


def iota(rows, lanes, axis):
    return lax.broadcasted_iota(jnp.int32, (rows, lanes), axis)


def where_one(test):
    return jnp.where(test, 1.0, 0.0).astype(F32)


def multiply(left, right):
    return jnp.dot(left, right, precision=HIGHEST, preferred_element_type=F32)


def pieces(value):
    first = value.astype(jnp.bfloat16)
    left = value - first.astype(F32)
    second = left.astype(jnp.bfloat16)
    third = (left - second.astype(F32)).astype(jnp.bfloat16)
    return first, second, third


def same_level():
    return (iota(128, 128, 0) & 3) == (iota(128, 128, 1) & 3)


def folded(product, place):
    pick = where_one((iota(32, 128, 1) >> 2) == iota(32, 128, 0))
    put = where_one((iota(128, 128, 0) >> 2) + 32 * place == iota(128, 128, 1))
    return multiply(multiply(pick, jnp.where(same_level(), product, 0.0)), put)


def packed(table):
    free = iota(8, 128, 1) >= 96
    return [
        jnp.where(free, pltpu.roll(table[24:32], 96 - 32 * part, 1), table[8 * part : 8 * part + 8])
        for part in range(3)
    ]


def unpacked(rows):
    group = iota(8, 128, 1) >> 5
    parts = [rows[8 * part : 8 * part + 8] for part in range(3)]
    moved = [pltpu.roll(parts[part], 32 + 32 * part, 1) for part in range(3)]
    last = jnp.where(group == 0, moved[0], jnp.where(group == 1, moved[1], moved[2]))
    return parts + [last]


def gram_kernel(matrix_ref, out_ref, pieces_ref):
    for index in range(12):
        lanes = slice(128 * index, 128 * index + 128)
        for place, piece in enumerate(pieces(matrix_ref[:, lanes])):
            pieces_ref[128 * place : 128 * place + 128, lanes] = piece
    matrix = matrix_ref[...]
    gram = lax.dot_general(matrix, matrix, (((1,), (1,)), ((), ())), precision=HIGHEST, preferred_element_type=F32)
    out_ref[...] = folded(gram, 0)


def gram_of(matrix):
    return pl.pallas_call(
        gram_kernel,
        out_shape=(shaped((32, 128)), jax.ShapeDtypeStruct((384, 1536), jnp.bfloat16)),
        name="gram",
        cost_estimate=cost(50000000, 2000000),
        compiler_params=params(),
    )(matrix)


def cross_kernel(own_ref, before_ref, after_ref, speeds_ref, matrix_ref, gram_ref, out_ref, ping, pong):
    first = 4 * lax.axis_index("tm")
    pick = where_one(iota(128, 128, 0) == first + (iota(128, 128, 1) & 3))
    coarse = advance(own_ref, before_ref, after_ref, multiply(speeds_ref[...], pick), ping, pong)
    cross = multiply(matrix_ref[...], coarse[:, 4:20].reshape(1536, 128))
    out_ref[...] = gram_ref[...] + folded(cross, 1)


def gram_and_cross(own, before, after, speeds, matrix, gram):
    return pl.pallas_call(
        cross_kernel,
        out_shape=shaped((32, 128)),
        scratch_shapes=[pltpu.VMEM((3, 24, 32, 128), F32)] * 2,
        name="gram_and_cross",
        cost_estimate=cost(18000000, 2800000),
        compiler_params=params(),
    )(own, before, after, speeds, matrix, gram)


def ends_kernel(chunks_ref, starts_ref, pair_ref, ends_ref, out_ref, split):
    for pair in range(6):
        rows = slice(8 * pair, 8 * pair + 8)
        blocks = from_chunks(chunks_ref[:, 0, rows, :], chunks_ref[:, 1, rows, :])
        for half in range(2):
            index = 2 * pair + half
            lanes = slice(128 * index, 128 * index + 128)
            ends_ref[:, lanes] = blocks[half]
            for place, piece in enumerate(pieces(blocks[half])):
                split[128 * place : 128 * place + 128, lanes] = piece

    def against(rows, columns):
        return lax.dot_general(
            starts_ref[0:rows], split[columns], (((1,), (1,)), ((), ())), preferred_element_type=F32
        )

    low, high = against(384, slice(0, 256)), against(128, slice(256, 384))
    product = (low[256:384, 0:128] + low[128:256, 128:256] + high) + (low[128:256, 0:128] + low[0:128, 128:256])
    product = product + low[0:128, 0:128]
    parts = packed(pair_ref[...] + folded(product, 2))
    for part in range(3):
        out_ref[:, 8 * part : 8 * part + 8, :] = jnp.broadcast_to(parts[part][None], (out_ref.shape[0], 8, 128))


def partial_sums(chunks, starts, pair, copies):
    return pl.pallas_call(
        ends_kernel,
        out_shape=(shaped((128, 1536)), shaped((copies, 24, 128))),
        scratch_shapes=[pltpu.VMEM((384, 1536), jnp.bfloat16)],
        name="partial_sums",
        cost_estimate=cost(50000000, 2800000), compiler_params=params(),
    )(chunks, starts, pair)


def total_kernel(parts_ref, out_ref):
    out_ref[...] = jnp.broadcast_to(jnp.sum(parts_ref[...], axis=0)[None], out_ref.shape)


def totals(parts, copies):
    return pl.pallas_call(
        total_kernel, out_shape=shaped((copies, 24, 128)), name="totals", cost_estimate=cost(100000, 600000), compiler_params=params()
    )(parts)


def eliminated(blocks):
    row = iota(8, 128, 0)
    for panel in range(4):
        columns = [
            [jnp.broadcast_to(block[:, 8 * panel + q : 8 * panel + q + 1], (8, 128)) for block in blocks]
            for q in range(8)
        ]
        for m in range(8):
            is_pivot = row == m
            column = columns[m]
            scale = 1.0 / column[panel][m : m + 1]

            def reduced(target):
                pivot = jnp.broadcast_to(target[panel][m : m + 1] * scale, (8, 128))
                return [
                    jnp.where(is_pivot, pivot, block - column[place] * pivot)
                    if place == panel
                    else block - column[place] * pivot
                    for place, block in enumerate(target)
                ]

            for q in range(m + 1, 8):
                columns[q] = reduced(columns[q])
            blocks = reduced(blocks)
    return blocks


def mixing_of(blocks):
    turned = jnp.concatenate(eliminated(blocks), axis=0).T
    power, moved = turned[32:64], turned[64:96]
    wide = multiply(power, where_one((iota(32, 128, 1) >> 2) == iota(32, 128, 0)))
    slice_of = iota(128, 32, 0) >> 2
    unit = where_one((slice_of == iota(128, 32, 1)) & (slice_of >= 1))
    change = multiply(where_one(slice_of == iota(128, 32, 1) + 1), moved) - unit

    def later(value, rows):
        return jnp.concatenate([jnp.zeros((rows, 32), F32), value[: 128 - rows]], axis=0)

    for level in range(5):
        change = change + multiply(later(change, 4 << level), power)
        if level < 4:
            power = multiply(power, power)
    return jnp.where(same_level(), multiply(later(change, 4), wide), 0.0)


def fresh_kernel(parts_ref, starts_ref, pieces_ref, ends_ref, out_ref, held, sems):
    one, two, three = pieces(mixing_of(unpacked(jnp.sum(parts_ref[...], axis=0))))
    mixing = jnp.concatenate([three, two, one, two, one, one], axis=1)
    first = iota(128, 256, 0) < 4
    copies = []
    for pair in range(6):
        columns = slice(256 * pair, 256 * pair + 256)
        starts = starts_ref[:, columns]
        prior = jnp.where(first, starts, pltpu.roll(ends_ref[:, columns], 4, 0))
        split = [pieces_ref[128 * place : 128 * place + 128, columns] for place in range(3)]
        split = jnp.concatenate([split[0], split[1], split[2], split[0], split[1], split[0]], axis=0)
        fresh = prior + jnp.dot(mixing, split, preferred_element_type=F32)
        even, odd = to_chunks(fresh[:, 0:128], fresh[:, 128:256])
        rows = slice(8 * pair, 8 * pair + 8)
        held[:, 0, rows, :] = even
        held[:, 1, rows, :] = odd
        copy = pltpu.make_async_copy(held.at[:, :, rows], out_ref.at[:, :, rows], sems.at[pair])
        copy.start()
        copies.append(copy)
    for copy in copies:
        copy.wait()


def fresh_chunks(parts, starts, split, ends):
    return pl.pallas_call(
        fresh_kernel,
        out_shape=shaped((16, 2, 48, 128)),
        in_specs=[pl.BlockSpec(memory_space=pltpu.VMEM)] * 4,
        out_specs=pl.BlockSpec(memory_space=pl.ANY),
        scratch_shapes=[pltpu.VMEM((16, 2, 48, 128), F32), pltpu.SemaphoreType.DMA((6,))],
        name="fresh_chunks",
        cost_estimate=cost(50000000, 2800000), compiler_params=params(),
    )(parts, starts, split, ends)


def exchanged(chunks):
    moved = lax.all_to_all(chunks.reshape(32, 48, 128), "tm", split_axis=0, concat_axis=0, tiled=True)
    return moved.reshape(16, 2, 48, 128)


def sides(first, last):
    size = lax.axis_size("space")
    up = [(i, (i + 1) % size) for i in range(size)]
    down = [(j, i) for i, j in up]
    return lax.ppermute(last, "space", up), lax.ppermute(first, "space", down)


def on_device(slice_starts, fine_ends, level_speeds):
    space = lax.axis_size("space")
    starts, ends = slice_starts[0], fine_ends[0]
    start_chunks = exchanged(chunked(starts, PAUSE))
    end_chunks = exchanged(chunked(ends))
    before, after = sides(starts[:, :STEPS], starts[:, -STEPS:])
    fine_jumps = fine_jumps_of(starts, before, after, level_speeds, ends)
    matrix, slab, first, last = slabbed(start_chunks)
    slab_before, slab_after = sides(first, last)
    gram, split = gram_of(matrix)
    pair = gram_and_cross(slab, slab_before, slab_after, level_speeds, matrix, gram)
    end_matrix, parts = partial_sums(end_chunks, split, pair, 32)
    parts = lax.all_to_all(parts, "tm", split_axis=0, concat_axis=0, tiled=True)
    parts = totals(parts, space)
    parts = lax.all_to_all(parts, "space", split_axis=0, concat_axis=0, tiled=True)
    new_starts = unchunked(exchanged(fresh_chunks(parts, matrix, split, end_matrix)))
    return new_starts[None], fine_jumps[None]


def solution(mesh):
    in_specs = (P("tm", None, "space", None, None), P("tm", None, "space", None, None), P())
    out_specs = (P("tm", None, "space", None, None), P("tm", None, "space", None, None))
    return jax.shard_map(
        on_device, mesh=mesh, in_specs=in_specs, out_specs=out_specs, check_vma=False
    )
```

```python
import functools

import jax
import jax.numpy as jnp
from jax import lax
from jax.experimental import pallas as pl
from jax.experimental.pallas import tpu as pltpu
from jax.sharding import PartitionSpec as P

STEPS = 4
SOUND = 0.15
DIFFUSION = 0.08
HIGHEST = lax.Precision.HIGHEST
F32 = jnp.float32
PAUSE = 10500


def shaped(shape):
    return jax.ShapeDtypeStruct(shape, F32)


def cost(flops, nbytes):
    return pl.CostEstimate(flops=flops, bytes_accessed=nbytes, transcendentals=0)


def params(limit=16 << 20):
    return pltpu.CompilerParams(vmem_limit_bytes=limit)


def low_half():
    return lax.broadcasted_iota(jnp.int32, (16, 8, 128), 1) < 4


def to_chunks(first, second):
    one, two = first.reshape(16, 8, 128), second.reshape(16, 8, 128)
    low = low_half()
    even = jnp.where(low, one, pltpu.roll(two, 4, 1))
    odd = jnp.where(low, pltpu.roll(one, 4, 1), two)
    return even, odd


def from_chunks(even, odd):
    low = low_half()
    one = jnp.where(low, even, pltpu.roll(odd, 4, 1))
    two = jnp.where(low, pltpu.roll(even, 4, 1), odd)
    return one.reshape(128, 128), two.reshape(128, 128)


def chunk_kernel(pause, tile_ref, out_ref, tile, held, in_sems, out_sems):
    arriving = [pltpu.make_async_copy(tile_ref.at[field], tile.at[field], in_sems.at[field]) for field in range(3)]
    for copy in arriving:
        copy.start()
    if pause:

        @pl.when(lax.rem(lax.axis_index("space"), 2) == 1)
        def _():
            pl.delay(pause)

    leaving = []
    for pair in range(6):
        if pair % 2 == 0:
            arriving[pair // 2].wait()
        blocks = []
        for half in range(2):
            field, part = divmod(2 * pair + half, 4)
            blocks.append(tile[field, 4 * part : 4 * part + 4].reshape(128, 128).T)
        rows = slice(8 * pair, 8 * pair + 8)
        even, odd = to_chunks(blocks[0], blocks[1])
        held[:, 0, rows, :] = even
        held[:, 1, rows, :] = odd
        copy = pltpu.make_async_copy(held.at[:, :, rows], out_ref.at[:, :, rows], out_sems.at[pair])
        copy.start()
        leaving.append(copy)
    for copy in leaving:
        copy.wait()


def chunked(tile, pause=0):
    return pl.pallas_call(
        functools.partial(chunk_kernel, pause),
        out_shape=shaped((16, 2, 48, 128)),
        in_specs=[pl.BlockSpec(memory_space=pltpu.HBM)],
        out_specs=pl.BlockSpec(memory_space=pltpu.HBM),
        scratch_shapes=[
            pltpu.VMEM((3, 16, 32, 128), F32),
            pltpu.VMEM((16, 2, 48, 128), F32),
            pltpu.SemaphoreType.DMA((3,)),
            pltpu.SemaphoreType.DMA((6,)),
        ],
        name="chunked",
        cost_estimate=cost(0, 1600000),
        compiler_params=params(67000000) if pause else params(),
    )(tile)


def unchunk_kernel(chunks_ref, out_ref, held, sems):
    leaving = []
    for pair in range(6):
        rows = slice(8 * pair, 8 * pair + 8)
        blocks = from_chunks(chunks_ref[:, 0, rows, :], chunks_ref[:, 1, rows, :])
        field, part = divmod(2 * pair, 4)
        for half in range(2):
            layer = 4 * (part + half)
            held[field, layer : layer + 4] = blocks[half].T.reshape(4, 32, 128)
        layers = slice(4 * part, 4 * part + 8)
        copy = pltpu.make_async_copy(held.at[field, layers], out_ref.at[field, layers], sems.at[pair])
        copy.start()
        leaving.append(copy)
    for copy in leaving:
        copy.wait()


def unchunked(chunks):
    return pl.pallas_call(
        unchunk_kernel,
        out_shape=shaped((3, 16, 32, 128)),
        in_specs=[pl.BlockSpec(memory_space=pltpu.VMEM)],
        out_specs=pl.BlockSpec(memory_space=pltpu.HBM),
        scratch_shapes=[pltpu.VMEM((3, 16, 32, 128), F32), pltpu.SemaphoreType.DMA((6,))],
        name="unchunked",
        cost_estimate=cost(0, 1600000),
        compiler_params=params(),
    )(chunks)


def slab_kernel(chunks_ref, matrix_ref, slab_ref, first_ref, last_ref):
    for pair in range(6):
        rows = slice(8 * pair, 8 * pair + 8)
        blocks = from_chunks(chunks_ref[:, 0, rows, :], chunks_ref[:, 1, rows, :])
        for half in range(2):
            index = 2 * pair + half
            field, part = divmod(index, 4)
            matrix_ref[:, 128 * index : 128 * index + 128] = blocks[half]
            turned = blocks[half].T.reshape(4, 32, 128)
            slab_ref[field, 4 * part : 4 * part + 4] = turned
            if part == 0:
                first_ref[field] = turned
            if part == 3:
                last_ref[field] = turned


def slabbed(chunks):
    edge = (3, STEPS, 32, 128)
    return pl.pallas_call(
        slab_kernel,
        out_shape=(shaped((128, 1536)), shaped((3, 16, 32, 128)), shaped(edge), shaped(edge)),
        name="slabbed",
        cost_estimate=cost(0, 2800000), compiler_params=params(),
    )(chunks)


def advance(own_ref, before_ref, after_ref, speeds, ping, pong):
    ping[:, 0:4] = before_ref[...]
    ping[:, 4:20] = own_ref[...]
    ping[:, 20:24] = after_ref[...]
    drift_x, drift_y = 0.5 * speeds[0:1], 0.5 * speeds[1:2]
    held, fresh = ping, pong
    for step in range(STEPS):

        def layer(place, _, held=held, fresh=fresh):
            centre, east, west = held[:, place], held[:, place + 1], held[:, place - 1]
            north = pltpu.roll(centre, 31, 1)
            south = pltpu.roll(centre, 1, 1)
            diff_x, diff_y = east - west, north - south
            around = (east + west) + (north + south)
            moved = (1.0 - 4.0 * DIFFUSION) * centre + DIFFUSION * around - drift_x * diff_x - drift_y * diff_y
            half = 0.5 * SOUND
            fresh[0, place] = moved[0] - half * (diff_x[1] + diff_y[2])
            fresh[1, place] = moved[1] - half * diff_x[0]
            fresh[2, place] = moved[2] - half * diff_y[0]
            return 0

        lax.fori_loop(step + 1, 23 - step, layer, 0)
        held, fresh = fresh, held
    return held


def jump_kernel(own_ref, before_ref, after_ref, speeds_ref, ends_ref, out_ref, ping, pong):
    coarse = advance(own_ref, before_ref, after_ref, speeds_ref[...], ping, pong)
    out_ref[...] = ends_ref[...] - coarse[:, 4:20]


def fine_jumps_of(own, before, after, speeds, ends):
    return pl.pallas_call(
        jump_kernel,
        out_shape=shaped((3, 16, 32, 128)),
        scratch_shapes=[pltpu.VMEM((3, 24, 32, 128), F32)] * 2,
        name="fine_jumps",
        cost_estimate=cost(18000000, 2800000), compiler_params=params(),
    )(own, before, after, speeds, ends)


def iota(rows, lanes, axis):
    return lax.broadcasted_iota(jnp.int32, (rows, lanes), axis)


def where_one(test):
    return jnp.where(test, 1.0, 0.0).astype(F32)


def multiply(left, right):
    return jnp.dot(left, right, precision=HIGHEST, preferred_element_type=F32)


def pieces(value):
    first = value.astype(jnp.bfloat16)
    left = value - first.astype(F32)
    second = left.astype(jnp.bfloat16)
    third = (left - second.astype(F32)).astype(jnp.bfloat16)
    return first, second, third


def same_level():
    return (iota(128, 128, 0) & 3) == (iota(128, 128, 1) & 3)


def folded(product, place):
    pick = where_one((iota(32, 128, 1) >> 2) == iota(32, 128, 0))
    put = where_one((iota(128, 128, 0) >> 2) + 32 * place == iota(128, 128, 1))
    return multiply(multiply(pick, jnp.where(same_level(), product, 0.0)), put)


def packed(table):
    free = iota(8, 128, 1) >= 96
    return [
        jnp.where(free, pltpu.roll(table[24:32], 96 - 32 * part, 1), table[8 * part : 8 * part + 8])
        for part in range(3)
    ]


def unpacked(rows):
    group = iota(8, 128, 1) >> 5
    parts = [rows[8 * part : 8 * part + 8] for part in range(3)]
    moved = [pltpu.roll(parts[part], 32 + 32 * part, 1) for part in range(3)]
    last = jnp.where(group == 0, moved[0], jnp.where(group == 1, moved[1], moved[2]))
    return parts + [last]


def gram_kernel(matrix_ref, out_ref, pieces_ref):
    for index in range(12):
        lanes = slice(128 * index, 128 * index + 128)
        for place, piece in enumerate(pieces(matrix_ref[:, lanes])):
            pieces_ref[128 * place : 128 * place + 128, lanes] = piece
    matrix = matrix_ref[...]
    gram = lax.dot_general(matrix, matrix, (((1,), (1,)), ((), ())), precision=HIGHEST, preferred_element_type=F32)
    out_ref[...] = folded(gram, 0)


def gram_of(matrix):
    return pl.pallas_call(
        gram_kernel,
        out_shape=(shaped((32, 128)), jax.ShapeDtypeStruct((384, 1536), jnp.bfloat16)),
        name="gram",
        cost_estimate=cost(50000000, 2000000),
        compiler_params=params(),
    )(matrix)


def cross_kernel(own_ref, before_ref, after_ref, speeds_ref, matrix_ref, gram_ref, out_ref, ping, pong):
    first = 4 * lax.axis_index("tm")
    pick = where_one(iota(128, 128, 0) == first + (iota(128, 128, 1) & 3))
    coarse = advance(own_ref, before_ref, after_ref, multiply(speeds_ref[...], pick), ping, pong)
    cross = multiply(matrix_ref[...], coarse[:, 4:20].reshape(1536, 128))
    out_ref[...] = gram_ref[...] + folded(cross, 1)


def gram_and_cross(own, before, after, speeds, matrix, gram):
    return pl.pallas_call(
        cross_kernel,
        out_shape=shaped((32, 128)),
        scratch_shapes=[pltpu.VMEM((3, 24, 32, 128), F32)] * 2,
        name="gram_and_cross",
        cost_estimate=cost(18000000, 2800000),
        compiler_params=params(),
    )(own, before, after, speeds, matrix, gram)


def ends_kernel(chunks_ref, starts_ref, pair_ref, ends_ref, out_ref, split):
    for pair in range(6):
        rows = slice(8 * pair, 8 * pair + 8)
        blocks = from_chunks(chunks_ref[:, 0, rows, :], chunks_ref[:, 1, rows, :])
        for half in range(2):
            index = 2 * pair + half
            lanes = slice(128 * index, 128 * index + 128)
            ends_ref[:, lanes] = blocks[half]
            for place, piece in enumerate(pieces(blocks[half])):
                split[128 * place : 128 * place + 128, lanes] = piece

    def against(rows, columns):
        return lax.dot_general(
            starts_ref[0:rows], split[columns], (((1,), (1,)), ((), ())), preferred_element_type=F32
        )

    low, high = against(384, slice(0, 256)), against(128, slice(256, 384))
    product = (low[256:384, 0:128] + low[128:256, 128:256] + high) + (low[128:256, 0:128] + low[0:128, 128:256])
    product = product + low[0:128, 0:128]
    parts = packed(pair_ref[...] + folded(product, 2))
    for part in range(3):
        out_ref[:, 8 * part : 8 * part + 8, :] = jnp.broadcast_to(parts[part][None], (out_ref.shape[0], 8, 128))


def partial_sums(chunks, starts, pair, copies):
    return pl.pallas_call(
        ends_kernel,
        out_shape=(shaped((128, 1536)), shaped((copies, 24, 128))),
        scratch_shapes=[pltpu.VMEM((384, 1536), jnp.bfloat16)],
        name="partial_sums",
        cost_estimate=cost(50000000, 2800000), compiler_params=params(),
    )(chunks, starts, pair)


def total_kernel(parts_ref, out_ref):
    out_ref[...] = jnp.broadcast_to(jnp.sum(parts_ref[...], axis=0)[None], out_ref.shape)


def totals(parts, copies):
    return pl.pallas_call(
        total_kernel, out_shape=shaped((copies, 24, 128)), name="totals", cost_estimate=cost(100000, 600000), compiler_params=params()
    )(parts)


def eliminated(blocks):
    row = iota(8, 128, 0)
    for panel in range(4):
        columns = [
            [jnp.broadcast_to(block[:, 8 * panel + q : 8 * panel + q + 1], (8, 128)) for block in blocks]
            for q in range(8)
        ]
        for m in range(8):
            is_pivot = row == m
            column = columns[m]
            scale = 1.0 / column[panel][m : m + 1]

            def reduced(target):
                pivot = jnp.broadcast_to(target[panel][m : m + 1] * scale, (8, 128))
                return [
                    jnp.where(is_pivot, pivot, block - column[place] * pivot)
                    if place == panel
                    else block - column[place] * pivot
                    for place, block in enumerate(target)
                ]

            for q in range(m + 1, 8):
                columns[q] = reduced(columns[q])
            blocks = reduced(blocks)
    return blocks


def mixing_of(blocks):
    turned = jnp.concatenate(eliminated(blocks), axis=0).T
    power, moved = turned[32:64], turned[64:96]
    wide = multiply(power, where_one((iota(32, 128, 1) >> 2) == iota(32, 128, 0)))
    slice_of = iota(128, 32, 0) >> 2
    unit = where_one((slice_of == iota(128, 32, 1)) & (slice_of >= 1))
    change = multiply(where_one(slice_of == iota(128, 32, 1) + 1), moved) - unit

    def later(value, rows):
        return jnp.concatenate([jnp.zeros((rows, 32), F32), value[: 128 - rows]], axis=0)

    for level in range(5):
        change = change + multiply(later(change, 4 << level), power)
        if level < 4:
            power = multiply(power, power)
    return jnp.where(same_level(), multiply(later(change, 4), wide), 0.0)


def fresh_kernel(parts_ref, starts_ref, pieces_ref, ends_ref, out_ref, held, sems):
    one, two, three = pieces(mixing_of(unpacked(jnp.sum(parts_ref[...], axis=0))))
    mixing = jnp.concatenate([three, two, one, two, one, one], axis=1)
    first = iota(128, 256, 0) < 4
    copies = []
    for pair in range(6):
        columns = slice(256 * pair, 256 * pair + 256)
        starts = starts_ref[:, columns]
        prior = jnp.where(first, starts, pltpu.roll(ends_ref[:, columns], 4, 0))
        split = [pieces_ref[128 * place : 128 * place + 128, columns] for place in range(3)]
        split = jnp.concatenate([split[0], split[1], split[2], split[0], split[1], split[0]], axis=0)
        fresh = prior + jnp.dot(mixing, split, preferred_element_type=F32)
        even, odd = to_chunks(fresh[:, 0:128], fresh[:, 128:256])
        rows = slice(8 * pair, 8 * pair + 8)
        held[:, 0, rows, :] = even
        held[:, 1, rows, :] = odd
        copy = pltpu.make_async_copy(held.at[:, :, rows], out_ref.at[:, :, rows], sems.at[pair])
        copy.start()
        copies.append(copy)
    for copy in copies:
        copy.wait()


def fresh_chunks(parts, starts, split, ends):
    return pl.pallas_call(
        fresh_kernel,
        out_shape=shaped((16, 2, 48, 128)),
        in_specs=[pl.BlockSpec(memory_space=pltpu.VMEM)] * 4,
        out_specs=pl.BlockSpec(memory_space=pl.ANY),
        scratch_shapes=[pltpu.VMEM((16, 2, 48, 128), F32), pltpu.SemaphoreType.DMA((6,))],
        name="fresh_chunks",
        cost_estimate=cost(50000000, 2800000), compiler_params=params(),
    )(parts, starts, split, ends)


def exchanged(chunks):
    moved = lax.all_to_all(chunks.reshape(32, 48, 128), "tm", split_axis=0, concat_axis=0, tiled=True)
    return moved.reshape(16, 2, 48, 128)


def sides(first, last):
    size = lax.axis_size("space")
    up = [(i, (i + 1) % size) for i in range(size)]
    down = [(j, i) for i, j in up]
    return lax.ppermute(last, "space", up), lax.ppermute(first, "space", down)


def on_device(slice_starts, fine_ends, level_speeds):
    space = lax.axis_size("space")
    starts, ends = slice_starts[0], fine_ends[0]
    start_chunks = exchanged(chunked(starts, PAUSE))
    end_chunks = exchanged(chunked(ends))
    before, after = sides(starts[:, :STEPS], starts[:, -STEPS:])
    fine_jumps = fine_jumps_of(starts, before, after, level_speeds, ends)
    matrix, slab, first, last = slabbed(start_chunks)
    slab_before, slab_after = sides(first, last)
    gram, split = gram_of(matrix)
    pair = gram_and_cross(slab, slab_before, slab_after, level_speeds, matrix, gram)
    end_matrix, parts = partial_sums(end_chunks, split, pair, 32)
    parts = lax.all_to_all(parts, "tm", split_axis=0, concat_axis=0, tiled=True)
    parts = totals(parts, space)
    parts = lax.all_to_all(parts, "space", split_axis=0, concat_axis=0, tiled=True)
    new_starts = unchunked(exchanged(fresh_chunks(parts, matrix, split, end_matrix)))
    return new_starts[None], fine_jumps[None]


def solution(mesh):
    in_specs = (P("tm", None, "space", None, None), P("tm", None, "space", None, None), P())
    out_specs = (P("tm", None, "space", None, None), P("tm", None, "space", None, None))
    return jax.shard_map(
        on_device, mesh=mesh, in_specs=in_specs, out_specs=out_specs, check_vma=False
    )
```

```python
import functools

import jax
import jax.numpy as jnp
from jax import lax
from jax.experimental import pallas as pl
from jax.experimental.pallas import tpu as pltpu
from jax.sharding import PartitionSpec as P

STEPS = 4
SOUND = 0.15
DIFFUSION = 0.08
HIGHEST = lax.Precision.HIGHEST
F32 = jnp.float32
PAUSE = 10500


def shaped(shape):
    return jax.ShapeDtypeStruct(shape, F32)


def cost(flops, nbytes):
    return pl.CostEstimate(flops=flops, bytes_accessed=nbytes, transcendentals=0)


def params(limit=16 << 20):
    return pltpu.CompilerParams(vmem_limit_bytes=limit)


def low_half():
    return lax.broadcasted_iota(jnp.int32, (16, 8, 128), 1) < 4


def to_chunks(first, second):
    one, two = first.reshape(16, 8, 128), second.reshape(16, 8, 128)
    low = low_half()
    even = jnp.where(low, one, pltpu.roll(two, 4, 1))
    odd = jnp.where(low, pltpu.roll(one, 4, 1), two)
    return even, odd


def from_chunks(even, odd):
    low = low_half()
    one = jnp.where(low, even, pltpu.roll(odd, 4, 1))
    two = jnp.where(low, pltpu.roll(even, 4, 1), odd)
    return one.reshape(128, 128), two.reshape(128, 128)


def chunk_kernel(pause, tile_ref, out_ref, tile, held, in_sems, out_sems):
    arriving = [pltpu.make_async_copy(tile_ref.at[field], tile.at[field], in_sems.at[field]) for field in range(3)]
    for copy in arriving:
        copy.start()
    if pause:

        @pl.when(lax.rem(lax.axis_index("space"), 2) == 1)
        def _():
            pl.delay(pause)

    leaving = []
    for pair in range(6):
        if pair % 2 == 0:
            arriving[pair // 2].wait()
        blocks = []
        for half in range(2):
            field, part = divmod(2 * pair + half, 4)
            blocks.append(tile[field, 4 * part : 4 * part + 4].reshape(128, 128).T)
        rows = slice(8 * pair, 8 * pair + 8)
        even, odd = to_chunks(blocks[0], blocks[1])
        held[:, 0, rows, :] = even
        held[:, 1, rows, :] = odd
        copy = pltpu.make_async_copy(held.at[:, :, rows], out_ref.at[:, :, rows], out_sems.at[pair])
        copy.start()
        leaving.append(copy)
    for copy in leaving:
        copy.wait()


def chunked(tile, pause=0):
    return pl.pallas_call(
        functools.partial(chunk_kernel, pause),
        out_shape=shaped((16, 2, 48, 128)),
        in_specs=[pl.BlockSpec(memory_space=pltpu.HBM)],
        out_specs=pl.BlockSpec(memory_space=pltpu.HBM),
        scratch_shapes=[
            pltpu.VMEM((3, 16, 32, 128), F32),
            pltpu.VMEM((16, 2, 48, 128), F32),
            pltpu.SemaphoreType.DMA((3,)),
            pltpu.SemaphoreType.DMA((6,)),
        ],
        name="chunked",
        cost_estimate=cost(0, 1600000),
        compiler_params=params(67000000) if pause else params(),
    )(tile)


def unchunk_kernel(chunks_ref, out_ref, held, sems):
    leaving = []
    for pair in range(6):
        rows = slice(8 * pair, 8 * pair + 8)
        blocks = from_chunks(chunks_ref[:, 0, rows, :], chunks_ref[:, 1, rows, :])
        field, part = divmod(2 * pair, 4)
        for half in range(2):
            layer = 4 * (part + half)
            held[field, layer : layer + 4] = blocks[half].T.reshape(4, 32, 128)
        layers = slice(4 * part, 4 * part + 8)
        copy = pltpu.make_async_copy(held.at[field, layers], out_ref.at[field, layers], sems.at[pair])
        copy.start()
        leaving.append(copy)
    for copy in leaving:
        copy.wait()


def unchunked(chunks):
    return pl.pallas_call(
        unchunk_kernel,
        out_shape=shaped((3, 16, 32, 128)),
        in_specs=[pl.BlockSpec(memory_space=pltpu.VMEM)],
        out_specs=pl.BlockSpec(memory_space=pltpu.HBM),
        scratch_shapes=[pltpu.VMEM((3, 16, 32, 128), F32), pltpu.SemaphoreType.DMA((6,))],
        name="unchunked",
        cost_estimate=cost(0, 1600000),
        compiler_params=params(),
    )(chunks)


def slab_kernel(chunks_ref, matrix_ref, slab_ref, first_ref, last_ref):
    for pair in range(6):
        rows = slice(8 * pair, 8 * pair + 8)
        blocks = from_chunks(chunks_ref[:, 0, rows, :], chunks_ref[:, 1, rows, :])
        for half in range(2):
            index = 2 * pair + half
            field, part = divmod(index, 4)
            matrix_ref[:, 128 * index : 128 * index + 128] = blocks[half]
            turned = blocks[half].T.reshape(4, 32, 128)
            slab_ref[field, 4 * part : 4 * part + 4] = turned
            if part == 0:
                first_ref[field] = turned
            if part == 3:
                last_ref[field] = turned


def slabbed(chunks):
    edge = (3, STEPS, 32, 128)
    return pl.pallas_call(
        slab_kernel,
        out_shape=(shaped((128, 1536)), shaped((3, 16, 32, 128)), shaped(edge), shaped(edge)),
        name="slabbed",
        cost_estimate=cost(0, 2800000), compiler_params=params(),
    )(chunks)


def advance(own_ref, before_ref, after_ref, speeds, ping, pong):
    ping[:, 0:4] = before_ref[...]
    ping[:, 4:20] = own_ref[...]
    ping[:, 20:24] = after_ref[...]
    drift_x, drift_y = 0.5 * speeds[0:1], 0.5 * speeds[1:2]
    held, fresh = ping, pong
    for step in range(STEPS):

        def layer(place, _, held=held, fresh=fresh):
            centre, east, west = held[:, place], held[:, place + 1], held[:, place - 1]
            north = pltpu.roll(centre, 31, 1)
            south = pltpu.roll(centre, 1, 1)
            diff_x, diff_y = east - west, north - south
            around = (east + west) + (north + south)
            moved = (1.0 - 4.0 * DIFFUSION) * centre + DIFFUSION * around - drift_x * diff_x - drift_y * diff_y
            half = 0.5 * SOUND
            fresh[0, place] = moved[0] - half * (diff_x[1] + diff_y[2])
            fresh[1, place] = moved[1] - half * diff_x[0]
            fresh[2, place] = moved[2] - half * diff_y[0]
            return 0

        lax.fori_loop(step + 1, 23 - step, layer, 0)
        held, fresh = fresh, held
    return held


def jump_kernel(own_ref, before_ref, after_ref, speeds_ref, ends_ref, out_ref, ping, pong):
    coarse = advance(own_ref, before_ref, after_ref, speeds_ref[...], ping, pong)
    out_ref[...] = ends_ref[...] - coarse[:, 4:20]


def fine_jumps_of(own, before, after, speeds, ends):
    return pl.pallas_call(
        jump_kernel,
        out_shape=shaped((3, 16, 32, 128)),
        scratch_shapes=[pltpu.VMEM((3, 24, 32, 128), F32)] * 2,
        name="fine_jumps",
        cost_estimate=cost(18000000, 2800000), compiler_params=params(),
    )(own, before, after, speeds, ends)


def iota(rows, lanes, axis):
    return lax.broadcasted_iota(jnp.int32, (rows, lanes), axis)


def where_one(test):
    return jnp.where(test, 1.0, 0.0).astype(F32)


def multiply(left, right):
    return jnp.dot(left, right, precision=HIGHEST, preferred_element_type=F32)


def pieces(value):
    first = value.astype(jnp.bfloat16)
    left = value - first.astype(F32)
    second = left.astype(jnp.bfloat16)
    third = (left - second.astype(F32)).astype(jnp.bfloat16)
    return first, second, third


def same_level():
    return (iota(128, 128, 0) & 3) == (iota(128, 128, 1) & 3)


def folded(product, place):
    pick = where_one((iota(32, 128, 1) >> 2) == iota(32, 128, 0))
    put = where_one((iota(128, 128, 0) >> 2) + 32 * place == iota(128, 128, 1))
    return multiply(multiply(pick, jnp.where(same_level(), product, 0.0)), put)


def packed(table):
    free = iota(8, 128, 1) >= 96
    return [
        jnp.where(free, pltpu.roll(table[24:32], 96 - 32 * part, 1), table[8 * part : 8 * part + 8])
        for part in range(3)
    ]


def unpacked(rows):
    group = iota(8, 128, 1) >> 5
    parts = [rows[8 * part : 8 * part + 8] for part in range(3)]
    moved = [pltpu.roll(parts[part], 32 + 32 * part, 1) for part in range(3)]
    last = jnp.where(group == 0, moved[0], jnp.where(group == 1, moved[1], moved[2]))
    return parts + [last]


def gram_kernel(matrix_ref, out_ref, pieces_ref):
    for index in range(12):
        lanes = slice(128 * index, 128 * index + 128)
        for place, piece in enumerate(pieces(matrix_ref[:, lanes])):
            pieces_ref[128 * place : 128 * place + 128, lanes] = piece
    matrix = matrix_ref[...]
    gram = lax.dot_general(matrix, matrix, (((1,), (1,)), ((), ())), precision=HIGHEST, preferred_element_type=F32)
    out_ref[...] = folded(gram, 0)


def gram_of(matrix):
    return pl.pallas_call(
        gram_kernel,
        out_shape=(shaped((32, 128)), jax.ShapeDtypeStruct((384, 1536), jnp.bfloat16)),
        name="gram",
        cost_estimate=cost(50000000, 2000000),
        compiler_params=params(),
    )(matrix)


def cross_kernel(own_ref, before_ref, after_ref, speeds_ref, matrix_ref, gram_ref, out_ref, ping, pong):
    first = 4 * lax.axis_index("tm")
    pick = where_one(iota(128, 128, 0) == first + (iota(128, 128, 1) & 3))
    coarse = advance(own_ref, before_ref, after_ref, multiply(speeds_ref[...], pick), ping, pong)
    cross = multiply(matrix_ref[...], coarse[:, 4:20].reshape(1536, 128))
    out_ref[...] = gram_ref[...] + folded(cross, 1)


def gram_and_cross(own, before, after, speeds, matrix, gram):
    return pl.pallas_call(
        cross_kernel,
        out_shape=shaped((32, 128)),
        scratch_shapes=[pltpu.VMEM((3, 24, 32, 128), F32)] * 2,
        name="gram_and_cross",
        cost_estimate=cost(18000000, 2800000),
        compiler_params=params(),
    )(own, before, after, speeds, matrix, gram)


def ends_kernel(chunks_ref, starts_ref, pair_ref, ends_ref, out_ref, split):
    for pair in range(6):
        rows = slice(8 * pair, 8 * pair + 8)
        blocks = from_chunks(chunks_ref[:, 0, rows, :], chunks_ref[:, 1, rows, :])
        for half in range(2):
            index = 2 * pair + half
            lanes = slice(128 * index, 128 * index + 128)
            ends_ref[:, lanes] = blocks[half]
            for place, piece in enumerate(pieces(blocks[half])):
                split[128 * place : 128 * place + 128, lanes] = piece

    def against(rows, columns):
        return lax.dot_general(
            starts_ref[0:rows], split[columns], (((1,), (1,)), ((), ())), preferred_element_type=F32
        )

    low, high = against(384, slice(0, 256)), against(128, slice(256, 384))
    product = (low[256:384, 0:128] + low[128:256, 128:256] + high) + (low[128:256, 0:128] + low[0:128, 128:256])
    product = product + low[0:128, 0:128]
    parts = packed(pair_ref[...] + folded(product, 2))
    for part in range(3):
        out_ref[:, 8 * part : 8 * part + 8, :] = jnp.broadcast_to(parts[part][None], (out_ref.shape[0], 8, 128))


def partial_sums(chunks, starts, pair, copies):
    return pl.pallas_call(
        ends_kernel,
        out_shape=(shaped((128, 1536)), shaped((copies, 24, 128))),
        scratch_shapes=[pltpu.VMEM((384, 1536), jnp.bfloat16)],
        name="partial_sums",
        cost_estimate=cost(50000000, 2800000), compiler_params=params(),
    )(chunks, starts, pair)


def total_kernel(parts_ref, out_ref):
    out_ref[...] = jnp.broadcast_to(jnp.sum(parts_ref[...], axis=0)[None], out_ref.shape)


def totals(parts, copies):
    return pl.pallas_call(
        total_kernel, out_shape=shaped((copies, 24, 128)), name="totals", cost_estimate=cost(100000, 600000), compiler_params=params()
    )(parts)


def eliminated(blocks):
    row = iota(8, 128, 0)
    for panel in range(4):
        columns = [
            [jnp.broadcast_to(block[:, 8 * panel + q : 8 * panel + q + 1], (8, 128)) for block in blocks]
            for q in range(8)
        ]
        for m in range(8):
            is_pivot = row == m
            column = columns[m]
            scale = 1.0 / column[panel][m : m + 1]

            def reduced(target):
                pivot = jnp.broadcast_to(target[panel][m : m + 1] * scale, (8, 128))
                return [
                    jnp.where(is_pivot, pivot, block - column[place] * pivot)
                    if place == panel
                    else block - column[place] * pivot
                    for place, block in enumerate(target)
                ]

            for q in range(m + 1, 8):
                columns[q] = reduced(columns[q])
            blocks = reduced(blocks)
    return blocks


def mixing_of(blocks):
    turned = jnp.concatenate(eliminated(blocks), axis=0).T
    power, moved = turned[32:64], turned[64:96]
    wide = multiply(power, where_one((iota(32, 128, 1) >> 2) == iota(32, 128, 0)))
    slice_of = iota(128, 32, 0) >> 2
    unit = where_one((slice_of == iota(128, 32, 1)) & (slice_of >= 1))
    change = multiply(where_one(slice_of == iota(128, 32, 1) + 1), moved) - unit

    def later(value, rows):
        return jnp.concatenate([jnp.zeros((rows, 32), F32), value[: 128 - rows]], axis=0)

    for level in range(4):
        change = change + multiply(later(change, 4 << level), power)
        power = multiply(power, power)
    whole = multiply(later(change, 4), wide) + multiply(later(change, 68), multiply(power, wide))
    return jnp.where(same_level(), whole, 0.0)


def fresh_kernel(parts_ref, starts_ref, pieces_ref, ends_ref, out_ref, held, sems):
    one, two, three = pieces(mixing_of(unpacked(jnp.sum(parts_ref[...], axis=0))))
    mixing = jnp.concatenate([three, two, one, two, one, one], axis=1)
    first = iota(128, 256, 0) < 4
    copies = []
    for pair in range(6):
        columns = slice(256 * pair, 256 * pair + 256)
        starts = starts_ref[:, columns]
        prior = jnp.where(first, starts, pltpu.roll(ends_ref[:, columns], 4, 0))
        split = [pieces_ref[128 * place : 128 * place + 128, columns] for place in range(3)]
        split = jnp.concatenate([split[0], split[1], split[2], split[0], split[1], split[0]], axis=0)
        fresh = prior + jnp.dot(mixing, split, preferred_element_type=F32)
        even, odd = to_chunks(fresh[:, 0:128], fresh[:, 128:256])
        rows = slice(8 * pair, 8 * pair + 8)
        held[:, 0, rows, :] = even
        held[:, 1, rows, :] = odd
        copy = pltpu.make_async_copy(held.at[:, :, rows], out_ref.at[:, :, rows], sems.at[pair])
        copy.start()
        copies.append(copy)
    for copy in copies:
        copy.wait()


def fresh_chunks(parts, starts, split, ends):
    return pl.pallas_call(
        fresh_kernel,
        out_shape=shaped((16, 2, 48, 128)),
        in_specs=[pl.BlockSpec(memory_space=pltpu.VMEM)] * 4,
        out_specs=pl.BlockSpec(memory_space=pl.ANY),
        scratch_shapes=[pltpu.VMEM((16, 2, 48, 128), F32), pltpu.SemaphoreType.DMA((6,))],
        name="fresh_chunks",
        cost_estimate=cost(50000000, 2800000), compiler_params=params(),
    )(parts, starts, split, ends)


def exchanged(chunks):
    moved = lax.all_to_all(chunks.reshape(32, 48, 128), "tm", split_axis=0, concat_axis=0, tiled=True)
    return moved.reshape(16, 2, 48, 128)


def sides(first, last):
    size = lax.axis_size("space")
    up = [(i, (i + 1) % size) for i in range(size)]
    down = [(j, i) for i, j in up]
    return lax.ppermute(last, "space", up), lax.ppermute(first, "space", down)


def on_device(slice_starts, fine_ends, level_speeds):
    space = lax.axis_size("space")
    starts, ends = slice_starts[0], fine_ends[0]
    start_chunks = exchanged(chunked(starts, PAUSE))
    end_chunks = exchanged(chunked(ends))
    before, after = sides(starts[:, :STEPS], starts[:, -STEPS:])
    fine_jumps = fine_jumps_of(starts, before, after, level_speeds, ends)
    matrix, slab, first, last = slabbed(start_chunks)
    slab_before, slab_after = sides(first, last)
    gram, split = gram_of(matrix)
    pair = gram_and_cross(slab, slab_before, slab_after, level_speeds, matrix, gram)
    end_matrix, parts = partial_sums(end_chunks, split, pair, 32)
    parts = lax.all_to_all(parts, "tm", split_axis=0, concat_axis=0, tiled=True)
    parts = totals(parts, space)
    parts = lax.all_to_all(parts, "space", split_axis=0, concat_axis=0, tiled=True)
    new_starts = unchunked(exchanged(fresh_chunks(parts, matrix, split, end_matrix)))
    return new_starts[None], fine_jumps[None]


def solution(mesh):
    in_specs = (P("tm", None, "space", None, None), P("tm", None, "space", None, None), P())
    out_specs = (P("tm", None, "space", None, None), P("tm", None, "space", None, None))
    return jax.shard_map(
        on_device, mesh=mesh, in_specs=in_specs, out_specs=out_specs, check_vma=False
    )
```
